256 devices in a mesh: ctx: 64 (over z, x_lo, y), kv: 4 (over x_hi, core).
Axes of the slice: x: 4 (x_hi: 2, x_lo: 2; x = x_hi * 2 + x_lo), y: 4, z: 8, core: 2. Of those that a mesh axis runs over, the one named last changes fastest.
Arguments:
- queries: float32 [2, 4096, 16384], P(None, 'ctx', 'kv'), may hold values from -5 to 5
- keys: float32 [2, 4096, 1024], P(None, 'ctx', 'kv'), may hold values from -5 to 5
- values: float32 [2, 4096, 1024], P(None, 'ctx', 'kv'), may hold values from -6 to 6
- query_maps: float32 [128, 128, 128], P('kv'), may hold values from -2.5 to 2.5
- key_maps: float32 [8, 128, 128], P('kv'), may hold values from -2.5 to 2.5
- mix: float32 [128], P('kv'), may hold values from -2 to 2
- window_blocks: int32 [2, 64], P(None, 'ctx'), may hold values from 0 to 255
- starts: int32 [2], replicated, may hold values from 0 to 1024, as said below
Outputs:
- attended: float32 [2, 4096, 16384], P(None, ('ctx', 'kv'))
The draws below stay inside these ranges and needn't reach their ends.
Inputs may be any that keep to these rules, and one draw needn't show every extreme that they name: Every start lies between 0 and 1024; some sequence starts exactly at 1024.
All inputs are finite; a program needn't handle non-finite values.
Results may differ from the reference program's by a relative error of at most 0.0003.
Values sent between devices are 32-bit elements; how exact they have to be, the bound alone decides.
A program may use at most 128 MiB of HBM per device.

```python
import jax
import jax.numpy as jnp
from jax import lax

QH = 128
KVH = 8
HD = 128
HALF = 128
BLOCK = 64
WBLK = 8
SEQS = 2
LENGTH = 4096
NBLK = 64


def draw_starts(key, part):
    first_key, second_key = jax.random.split(jax.random.fold_in(key, 11), 2)
    drawn = jax.random.randint(first_key, (SEQS,), 0, LENGTH // 4 + 1)
    chosen = jax.random.randint(second_key, (), 0, SEQS)
    index = jnp.arange(SEQS)
    return jnp.where(index == chosen, LENGTH // 4, drawn).astype(jnp.int32)


def plant_layout(key):
    base = jax.random.fold_in(key, 101)
    block_key, offset_key, head_key, sign_key = jax.random.split(base, 4)
    first = NBLK // 4
    count = min(8, NBLK - first)
    seq_keys = jax.random.split(block_key, SEQS)
    blocks = jax.vmap(lambda one_key: jax.random.permutation(one_key, NBLK - first)[:count])(seq_keys) + first
    offsets = jax.random.randint(offset_key, (SEQS, count), 2, BLOCK)
    heads = jax.random.randint(head_key, (SEQS, count), 0, QH)
    signs = (2 * jax.random.randint(sign_key, (SEQS, count, HD), 0, 2) - 1).astype(jnp.float32)
    levels = jnp.array([3.2, 4.2, 5.0], dtype=jnp.float32)
    strengths = levels[jnp.arange(count) % 3]
    positions = (blocks * BLOCK + offsets).astype(jnp.int32)
    return (positions, heads.astype(jnp.int32), signs, strengths)


def base_field(key, width):
    noise_key = jax.random.fold_in(key, 0)
    field = jax.random.normal(noise_key, (SEQS, LENGTH, width), jnp.float32)
    return jnp.clip(field, -4.0, 4.0)


def draw_queries(key, part):
    field = base_field(jax.random.fold_in(key, 7), QH * HD)
    positions, heads, signs, strengths = plant_layout(key)
    columns = heads[:, :, None] * HD + jnp.arange(HD, dtype=jnp.int32)[None, None, :]
    seq_index = jnp.arange(SEQS, dtype=jnp.int32)[:, None, None]
    planted = strengths[None, :, None] * signs
    return field.at[seq_index, positions[:, :, None], columns].set(planted)


def draw_keys(key, part):
    field = base_field(jax.random.fold_in(key, 9), KVH * HD)
    positions, heads, signs, strengths = plant_layout(key)
    kv_heads = heads // (QH // KVH)
    columns = kv_heads[:, :, None] * HD + jnp.arange(HD, dtype=jnp.int32)[None, None, :]
    seq_index = jnp.arange(SEQS, dtype=jnp.int32)[:, None, None]
    near_level = strengths[None, :, None] * signs
    lower = strengths - 2.0 / (strengths * HD ** 0.5)
    second_level = lower[None, :, None] * signs
    field = field.at[seq_index, positions[:, :, None] - 1, columns].set(near_level)
    return field.at[seq_index, positions[:, :, None] - 2, columns].set(second_level)


def set_ends(values, key, smallest, largest):
    spot = [jax.random.randint(jax.random.fold_in(key, axis), (), 0, length) for axis, length in enumerate(values.shape)]
    main_axis = values.shape.index(max(values.shape))
    neighbour = spot[:main_axis] + [(spot[main_axis] + 1) % values.shape[main_axis]] + spot[main_axis + 1:]
    return values.at[tuple(spot)].set(smallest).at[tuple(neighbour)].set(largest)


def block_scale(rng, extent, pieces, least, top_value):
    loudness = 1.0
    for dim, blocks in pieces:
        draws = jax.random.uniform(jax.random.fold_in(jax.random.fold_in(rng, 6), dim), (blocks,), jnp.float32, least / len(pieces), top_value / len(pieces))
        loudness = loudness * jnp.repeat(jnp.exp(draws), extent[dim] // blocks).reshape((-1,) + (1,) * (len(extent) - 1 - dim))
    return loudness


def scatter_about(rng, dims, scale, reach, pieces=(), held_as=jnp.bfloat16):
    factor_of = block_scale(rng, dims, pieces, -0.22, 0.18) if pieces else 1.0
    values = jax.random.normal(rng, dims, jnp.float32) * scale * factor_of
    return jnp.minimum(jnp.maximum(values, -reach), reach).astype(held_as)


def setup_inputs(seed: int = 0) -> dict:
    seeds = jax.random.split(jax.random.key(seed), 9)
    queries = draw_queries(jax.random.fold_in(seeds[8], 71), 0)
    keys = draw_keys(jax.random.fold_in(seeds[8], 71), 0)
    values = scatter_about(seeds[2], (SEQS, LENGTH, KVH * HD), 1.0, 6.0, ((1, 64), (2, 4)), jnp.float32)
    query_maps = scatter_about(seeds[3], (QH, HD, HALF), 0.25, 2.5, ((0, 4),), jnp.float32)
    key_maps = scatter_about(seeds[4], (KVH, HD, HALF), 0.25, 2.5, ((0, 4),), jnp.float32)
    mix = jnp.clip(jax.random.uniform(seeds[5], (QH,), jnp.float32, -2.0, 2.0) * block_scale(seeds[5], (QH,), ((0, 4),), -0.4, 0.0), -2.0, 2.0)
    window_blocks = set_ends(jax.random.randint(seeds[6], (SEQS, NBLK), 0, 256), jax.random.fold_in(seeds[6], 1), 0, 255).astype(jnp.int32)
    starts = draw_starts(jax.random.fold_in(seeds[8], 71), 0)
    return dict(queries=queries, keys=keys, values=values, query_maps=query_maps, key_maps=key_maps, mix=mix, window_blocks=window_blocks, starts=starts)


highest = lax.Precision.HIGHEST


def featurize(inputs, feature_maps):
    logits = jnp.einsum("...hd,hdf->...hf", inputs, feature_maps, precision=highest)
    upper_exp = jnp.exp(logits)
    lower_exp = jnp.exp(-logits)
    return jnp.concatenate([upper_exp / jnp.sum(upper_exp, axis=-1, keepdims=True), lower_exp / jnp.sum(lower_exp, axis=-1, keepdims=True)], axis=-1)


def window_mask(pattern_bits, key_live):
    window_len = (WBLK + 1) * BLOCK
    row_ids = jnp.arange(BLOCK, dtype=jnp.int32)[:, None]
    col_ids = jnp.arange(window_len, dtype=jnp.int32)[None, :]
    key_block = col_ids // BLOCK
    distance = WBLK - key_block
    divisor = jnp.power(2, jnp.maximum(distance - 1, 0)).astype(jnp.int32)
    picked = ((pattern_bits[:, :, None] // divisor) % 2) == 1
    causal = (col_ids - WBLK * BLOCK) <= row_ids
    allowed = jnp.where(key_block == WBLK, causal, picked)
    return allowed & key_live[:, None, :]


def attend_block(query_heads, key_rows, value_rows, allowed, rows_live, features_q, state_now, norm_now, weight):
    scores = jnp.einsum("sbkgd,swkd->skgbw", query_heads, key_rows, precision=highest) * (HD ** -0.5)
    chosen = allowed[:, None, None, :, :]
    row_peak = jnp.max(jnp.where(chosen, scores, -1e30), axis=-1, keepdims=True)
    exp_terms = jnp.where(chosen, jnp.exp(scores - row_peak), 0.0)
    near_sum = jnp.einsum("skgbw,swkd->sbkgd", exp_terms, value_rows, precision=highest)
    near_norm = jnp.einsum("skgbw->sbkg", exp_terms)
    far_sum = jnp.einsum("sbkgf,skfd->sbkgd", features_q, state_now, precision=highest)
    far_norm = jnp.einsum("sbkgf,skf->sbkg", features_q, norm_now, precision=highest)
    numerator = weight[:, :, None] * near_sum + (1.0 - weight[:, :, None]) * far_sum
    denominator = weight * near_norm + (1.0 - weight) * far_norm
    live_rows = rows_live[:, :, None, None]
    safe_den = jnp.where(live_rows, denominator, 1.0)
    attended = jnp.where(live_rows[..., None], numerator / safe_den[..., None], 0.0)
    return attended.reshape(attended.shape[0], attended.shape[1], -1)


def reference(queries, keys, values, query_maps, key_maps, mix, window_blocks, starts):
    seq_count, seq_length, query_width = queries.shape
    block_total = seq_length // BLOCK
    groups = QH // KVH
    features = 2 * HALF
    window_len = (WBLK + 1) * BLOCK
    positions = jnp.arange(seq_length, dtype=jnp.int32)
    live = positions[None, :] >= starts.astype(jnp.int32)[:, None]
    key_heads = keys.reshape(seq_count, seq_length, KVH, HD)
    value_heads = values.reshape(seq_count, seq_length, KVH, HD)
    key_features = jnp.where(live[:, :, None, None], featurize(key_heads, key_maps), 0.0)
    blocked_features = key_features.reshape(seq_count, block_total, BLOCK, KVH, features)
    blocked_values = value_heads.reshape(seq_count, block_total, BLOCK, KVH, HD)
    block_states = jnp.einsum("snbkf,snbkd->snkfd", blocked_features, blocked_values, precision=highest)
    block_norms = jnp.sum(blocked_features, axis=2)
    state_sums = jnp.cumsum(block_states, axis=1)
    norm_sums = jnp.cumsum(block_norms, axis=1)
    lead_blocks = WBLK + 1
    far_states = jnp.concatenate([jnp.zeros_like(state_sums[:, :lead_blocks]), state_sums[:, : block_total - lead_blocks]], axis=1)
    far_norms = jnp.concatenate([jnp.zeros_like(norm_sums[:, :lead_blocks]), norm_sums[:, : block_total - lead_blocks]], axis=1)
    pad_rows = WBLK * BLOCK
    key_padded = jnp.concatenate([jnp.zeros_like(key_heads[:, :pad_rows]), key_heads], axis=1)
    value_padded = jnp.concatenate([jnp.zeros_like(value_heads[:, :pad_rows]), value_heads], axis=1)
    live_padded = jnp.concatenate([jnp.zeros_like(live[:, :pad_rows]), live], axis=1)
    weight = jax.nn.sigmoid(mix).reshape(KVH, groups)

    def one_block(block_index):
        row_start = block_index * BLOCK
        query_rows = lax.dynamic_slice_in_dim(queries, row_start, BLOCK, 1).reshape(seq_count, BLOCK, QH, HD)
        features_q = featurize(query_rows, query_maps).reshape(seq_count, BLOCK, KVH, groups, features)
        key_rows = lax.dynamic_slice_in_dim(key_padded, row_start, window_len, 1)
        value_rows = lax.dynamic_slice_in_dim(value_padded, row_start, window_len, 1)
        key_live = lax.dynamic_slice_in_dim(live_padded, row_start, window_len, 1)
        pattern_bits = lax.dynamic_slice_in_dim(window_blocks, block_index, 1, 1)
        allowed = window_mask(pattern_bits, key_live)
        rows_live = lax.dynamic_slice_in_dim(live, row_start, BLOCK, 1)
        state_now = lax.dynamic_index_in_dim(far_states, block_index, 1, keepdims=False)
        norm_now = lax.dynamic_index_in_dim(far_norms, block_index, 1, keepdims=False)
        return attend_block(query_rows.reshape(seq_count, BLOCK, KVH, groups, HD), key_rows, value_rows, allowed, rows_live, features_q, state_now, norm_now, weight)

    outputs = lax.map(one_block, jnp.arange(block_total, dtype=jnp.int32))
    return jnp.moveaxis(outputs, 0, 1).reshape(seq_count, seq_length, query_width)
```

```python
import functools

import jax
import jax.numpy as jnp
from jax import lax
from jax.experimental import pallas as pl
from jax.experimental.pallas import tpu as pltpu
from jax.sharding import Mesh
from jax.sharding import PartitionSpec as P

HD = 128
HALF = 128
FEAT = 2 * HALF
BLOCK = 64
WBLK = 8
GROUP = 16
PLANE = 8
PLANES = 8
SEQS = 2
KVL = 2
COMBOS = SEQS * KVL
QL = KVL * GROUP * HD
WIN = 640
CHUNK = COMBOS * 16 + 8
NEG = -1e30
CTX = ("ctx_0", "ctx_1", "ctx_2")
KV = ("kv_0", "kv_1")
CTX_KV = CTX + KV
MESH = pl.DeviceIdType.MESH
F32 = jnp.float32
BF16 = jnp.bfloat16
HIGHEST = lax.Precision.HIGHEST

NN = (((1,), (0,)), ((), ()))
NT = (((1,), (1,)), ((), ()))
TN = (((0,), (0,)), ((), ()))


def remote(src, dst, send, recv, device):
    return pltpu.make_async_remote_copy(
        src_ref=src, dst_ref=dst, send_sem=send, recv_sem=recv, device_id=device, device_id_type=MESH
    )


def mm(a, b, dims):
    return lax.dot_general(a, b, dims, preferred_element_type=F32)


def split(x):
    hi = x.astype(BF16)
    return hi, (x - hi.astype(F32)).astype(BF16)


def softmax_pair(logits):
    up = jnp.exp(logits)
    down = jnp.exp(-logits)
    up = up / jnp.sum(up, axis=-1, keepdims=True)
    down = down / jnp.sum(down, axis=-1, keepdims=True)
    return jnp.concatenate([up, down], axis=-1)


def here():
    return [lax.axis_index(a) for a in CTX_KV]


def gather_kernel(
    k_ref, v_ref, kmap_ref, mask_ref, kwin, vwin, far,
    prev_k, prev_v, st, rs, zt, zr, zx, zp, own_sem, zs_sem, zr_sem, ks_sem, kr_sem,
    a_send, a_recv, b_send, b_recv, c_send, c_recv, d_send, d_recv,
):
    z, x, y, h, c = here()
    me = x * 4 + y

    def plane_peer(o):
        j = lax.rem(me + o, PLANE)
        return j, (z, j // 4, lax.rem(j, 4), h, c)

    def column_peer(o):
        j = lax.rem(z + o, PLANES)
        return j, (j, x, y, h, c)

    barrier = pltpu.get_barrier_semaphore()
    for o in range(1, PLANE):
        pl.semaphore_signal(barrier, inc=1, device_id=plane_peer(o)[1], device_id_type=MESH)
    for o in range(1, PLANES):
        pl.semaphore_signal(barrier, inc=1, device_id=column_peer(o)[1], device_id_type=MESH)
    pl.semaphore_wait(barrier, PLANE + PLANES - 2)

    above = column_peer(1)[1]
    shifts = [
        remote(k_ref, prev_k, zs_sem.at[0], zr_sem.at[0], above),
        remote(v_ref, prev_v, zs_sem.at[1], zr_sem.at[1], above),
    ]
    for copy in shifts:
        copy.start()

    def window_copies(o, k_src, v_src):
        device = plane_peer(o)[1]
        return (
            remote(k_src, kwin.at[me], ks_sem.at[0, o], kr_sem.at[0, me], device),
            remote(v_src, vwin.at[me], ks_sem.at[1, o], kr_sem.at[1, me], device),
        )

    for o in range(1, PLANE):
        @pl.when(me + o < PLANE)
        def _():
            for copy in window_copies(o, k_ref, v_ref):
                copy.start()

    shifts[0].wait_recv()
    phis = {}
    live = jnp.concatenate([mask_ref[0], mask_ref[1]], axis=0) > 0.0
    for g in range(KVL):
        rows = jnp.concatenate([prev_k[s, :, g * HD:(g + 1) * HD] for s in range(SEQS)], axis=0)
        logits = lax.dot_general(rows, kmap_ref[g], NN, precision=HIGHEST, preferred_element_type=F32)
        phi = softmax_pair(logits)
        phi = jnp.where(jnp.concatenate([live, live], axis=1), phi, 0.0)
        for s in range(SEQS):
            phis[s, g] = phi[s * BLOCK:(s + 1) * BLOCK]
    shifts[1].wait_recv()
    norms = []
    for s in range(SEQS):
        for g in range(KVL):
            phi = phis[s, g]
            value = prev_v[s, :, g * HD:(g + 1) * HD]
            state = lax.dot_general(value, phi, TN, precision=HIGHEST, preferred_element_type=F32)
            n = s * KVL + g
            for j in range(PLANE):
                st[j, n * 16:(n + 1) * 16, :] = state[j * 16:(j + 1) * 16, :]
            norms.append(jnp.sum(phi, axis=0, keepdims=True))
    norm_tile = jnp.concatenate(norms + [jnp.zeros((8 - COMBOS, FEAT), F32)], axis=0)
    for j in range(PLANE):
        st[j, COMBOS * 16:CHUNK, :] = norm_tile

    def a_copy(o):
        j, device = plane_peer(o)
        return remote(st.at[j], rs.at[me], a_send.at[o], a_recv.at[me], device)

    for o in range(1, PLANE):
        a_copy(o).start()

    for o in range(1, PLANE):
        @pl.when(me + o >= PLANE)
        def _():
            for copy in window_copies(o, prev_k, prev_v):
                copy.start()
    own = [
        pltpu.make_async_copy(prev_k, kwin.at[me], own_sem.at[0]),
        pltpu.make_async_copy(prev_v, vwin.at[me], own_sem.at[1]),
    ]
    for copy in own:
        copy.start()
    rs[me] = st[me]

    def from_peer(o, buf, send, recv):
        j = lax.rem(me - o + PLANE, PLANE)
        return remote(buf.at[j], buf.at[j], send.at[o], recv.at[j], plane_peer(o)[1])

    for o in range(1, PLANE):
        from_peer(o, rs, a_send, a_recv).wait_recv()
    total = jnp.zeros((CHUNK, FEAT), F32)
    for j in range(PLANE):
        part = rs[j]
        rs[j] = total
        total = total + part
    for j in range(PLANES):
        zt[j, 0:8, :] = total[j * 8:(j + 1) * 8]
        zt[j, 8:16, :] = total[COMBOS * 16:]

    def column_copy(o, src, dst, send, recv):
        j, device = column_peer(o)
        return remote(src.at[j], dst.at[z], send.at[o], recv.at[z], device)

    def from_column(o, buf, send, recv):
        j = lax.rem(z - o + PLANES, PLANES)
        return remote(buf.at[j], buf.at[j], send.at[o], recv.at[j], column_peer(o)[1])

    for o in range(1, PLANES):
        column_copy(o, zt, zr, b_send, b_recv).start()
    zr[z] = zt[z]
    for o in range(1, PLANES):
        from_column(o, zr, b_send, b_recv).wait_recv()
    running = jnp.zeros((16, FEAT), F32)
    for j in range(PLANES):
        zx[j] = running
        running = running + zr[j]
    for o in range(1, PLANES):
        column_copy(o, zx, zp, c_send, c_recv).start()
    zp[z] = zx[z]
    for o in range(1, PLANES):
        from_column(o, zp, c_send, c_recv).wait_recv()
    passed = jnp.concatenate([zp[j, 0:8, :] for j in range(PLANES)] + [zp[0, 8:16, :]], axis=0)
    for o in range(1, PLANE):
        a_copy(o).wait_send()
    for j in range(PLANE):
        st[j] = rs[j] + passed

    def d_copy(o):
        j, device = plane_peer(o)
        return remote(st.at[j], far.at[me], d_send.at[o], d_recv.at[me], device)

    for o in range(1, PLANE):
        d_copy(o).start()
    mine = pltpu.make_async_copy(st.at[me], far.at[me], own_sem.at[2])
    mine.start()

    for copy in shifts:
        copy.wait_send()
    for copy in own:
        copy.wait()
    for o in range(1, PLANE):
        for n, buf in enumerate((kwin, vwin)):
            j = lax.rem(me - o + PLANE, PLANE)
            copy = remote(k_ref, buf.at[j], ks_sem.at[n, o], kr_sem.at[n, j], plane_peer(o)[1])
            copy.wait_send()
            copy.wait_recv()
    for o in range(1, PLANES):
        column_copy(o, zt, zr, b_send, b_recv).wait_send()
        column_copy(o, zx, zp, c_send, c_recv).wait_send()
    mine.wait()
    for o in range(1, PLANE):
        from_peer(o, far, d_send, d_recv).wait()


def gather(keys, values, key_maps, mask):
    vmem = pl.BlockSpec(memory_space=pltpu.VMEM)
    hbm = pl.BlockSpec(memory_space=pl.ANY)
    dma = pltpu.SemaphoreType.DMA
    window = jax.ShapeDtypeStruct((PLANE,) + keys.shape, F32)
    return pl.pallas_call(
        gather_kernel,
        out_shape=(window, window, jax.ShapeDtypeStruct((PLANE, CHUNK, FEAT), F32)),
        in_specs=[vmem] * 4,
        out_specs=(hbm, hbm, hbm),
        scratch_shapes=[
            pltpu.VMEM(keys.shape, F32),
            pltpu.VMEM(keys.shape, F32),
            pltpu.VMEM((PLANE, CHUNK, FEAT), F32),
            pltpu.VMEM((PLANE, CHUNK, FEAT), F32),
            pltpu.VMEM((PLANES, 16, FEAT), F32),
            pltpu.VMEM((PLANES, 16, FEAT), F32),
            pltpu.VMEM((PLANES, 16, FEAT), F32),
            pltpu.VMEM((PLANES, 16, FEAT), F32),
            dma((3,)), dma((2,)), dma((2,)), dma((2, 8)), dma((2, 8)),
            dma((8,)), dma((8,)), dma((8,)), dma((8,)), dma((8,)), dma((8,)), dma((8,)), dma((8,)),
        ],
        name="gather",
        compiler_params=pltpu.CompilerParams(collective_id=0, has_side_effects=True),
    )(keys, values, key_maps, mask)


HEADS = 4


def attend_kernel(
    info_ref, weight_ref, q_ref, qmap_ref, k_ref, v_ref, kwin_ref, vwin_ref, far_ref, bias_ref, out_ref,
    k_hi, k_lo, v_hi, v_lo, f_hi, f_lo,
):
    g, s = pl.program_id(0), pl.program_id(1)
    zeros = jnp.zeros((WIN - (WBLK + 1) * BLOCK, HD), F32)
    keys = jnp.concatenate([kwin_ref[j, 0] for j in range(PLANE)] + [k_ref[0], zeros], axis=0)
    hi, lo = split(keys)
    k_hi[...] = jnp.concatenate([hi, hi], axis=1)
    k_lo[...] = jnp.concatenate([lo, lo], axis=1)
    vals = jnp.concatenate([vwin_ref[j, 0] for j in range(PLANE)] + [v_ref[0], zeros], axis=0)
    hi, lo = split(vals)
    v_hi[...] = jnp.concatenate([hi, jnp.ones((WIN, HD), BF16)], axis=1)
    v_lo[...] = lo
    n = s * KVL + g
    state = jnp.concatenate([far_ref[j, pl.ds(pl.multiple_of(n * 16, 16), 16), :] for j in range(PLANE)], axis=0)
    norm = far_ref[0, pl.ds(COMBOS * 16 + n, 1), :]
    hi, lo = split(jnp.concatenate([state, jnp.broadcast_to(norm, (HD, FEAT))], axis=0))
    f_hi[...] = hi
    f_lo[...] = lo
    row = lax.broadcasted_iota(jnp.int32, (BLOCK, HD), 0)
    col = lax.broadcasted_iota(jnp.int32, (BLOCK, HD), 1)
    bias = bias_ref[0]
    own_bias = jnp.where(col <= row, bias[:1, WBLK * BLOCK:], NEG)
    own_bias = jnp.concatenate([own_bias] * HEADS, axis=0)
    live = (row + info_ref[SEQS]) >= info_ref[s]

    @pl.loop(0, GROUP // HEADS)
    def _(step):
        wide = q_ref[0, :, pl.ds(pl.multiple_of(step * HEADS * HD, HEADS * HD), HEADS * HD)]
        logits = []
        rows = []
        for n in range(HEADS):
            x = wide[:, n * HD:(n + 1) * HD]
            rows.append(x)
            x_hi, x_lo = split(x)
            w_hi, w_lo = split(qmap_ref[step * HEADS + n])
            w = jnp.concatenate([w_hi, w_lo], axis=1)
            both = mm(jnp.concatenate([x_hi, x_lo], axis=1), jnp.concatenate([w, w], axis=0), NN)
            logits.append(both[:, :HALF] + both[:, HALF:])
        phi = softmax_pair(jnp.concatenate(logits, axis=0))
        p_hi, p_lo = split(phi)
        far = mm(p_hi, f_hi[...], NT) + mm(p_lo, f_hi[...], NT) + mm(p_hi, f_lo[...], NT)
        q_hi, q_lo = split(jnp.concatenate(rows, axis=0) * HD ** -0.5)
        q = jnp.concatenate([q_hi, q_lo], axis=1)
        scores = mm(q, k_hi[...], NT) + mm(q, k_lo[...], NT)
        scores = jnp.concatenate(
            [scores[:, :WBLK * BLOCK] + bias[:1, :WBLK * BLOCK], scores[:, WBLK * BLOCK:] + own_bias], axis=1
        )
        top = jnp.max(scores, axis=1, keepdims=True)
        e_hi, e_lo = split(jnp.exp(scores - top))
        near = mm(e_hi, v_hi[...], NN) + mm(e_lo, v_hi[...], NN)
        extra = mm(e_hi, v_lo[...], NN)
        for n in range(HEADS):
            a = weight_ref[(g * GROUP + step * HEADS + n)]
            part = slice(n * BLOCK, (n + 1) * BLOCK)
            top_part = a * (near[part, :HD] + extra[part]) + (1.0 - a) * far[part, :HD]
            bottom = a * near[part, HD:] + (1.0 - a) * far[part, HD:]
            result = jnp.where(live, top_part / jnp.where(live, bottom, 1.0), 0.0)
            out_ref[0, :, pl.ds(pl.multiple_of((step * HEADS + n) * HD, HD), HD)] = result


def attend(info, weight, queries, query_maps, keys, values, kwin, vwin, far, bias):
    smem = pl.BlockSpec(memory_space=pltpu.SMEM)
    return pl.pallas_call(
        attend_kernel,
        grid=(KVL, SEQS),
        out_shape=jax.ShapeDtypeStruct((SEQS, BLOCK, QL), F32),
        in_specs=[
            smem,
            smem,
            pl.BlockSpec((1, BLOCK, GROUP * HD), lambda g, s: (s, 0, g)),
            pl.BlockSpec((GROUP, HD, HALF), lambda g, s: (g, 0, 0)),
            pl.BlockSpec((1, BLOCK, HD), lambda g, s: (s, 0, g)),
            pl.BlockSpec((1, BLOCK, HD), lambda g, s: (s, 0, g)),
            pl.BlockSpec((PLANE, 1, BLOCK, HD), lambda g, s: (0, s, 0, g)),
            pl.BlockSpec((PLANE, 1, BLOCK, HD), lambda g, s: (0, s, 0, g)),
            pl.BlockSpec((PLANE, CHUNK, FEAT), lambda g, s: (0, 0, 0)),
            pl.BlockSpec((1, 8, WIN), lambda g, s: (s, 0, 0)),
        ],
        out_specs=pl.BlockSpec((1, BLOCK, GROUP * HD), lambda g, s: (s, 0, g)),
        scratch_shapes=[
            pltpu.VMEM((WIN, 2 * HD), BF16),
            pltpu.VMEM((WIN, 2 * HD), BF16),
            pltpu.VMEM((WIN, 2 * HD), BF16),
            pltpu.VMEM((WIN, HD), BF16),
            pltpu.VMEM((2 * HD, FEAT), BF16),
            pltpu.VMEM((2 * HD, FEAT), BF16),
        ],
        name="attend",
        compiler_params=pltpu.CompilerParams(vmem_limit_bytes=48 << 20),
    )(info, weight, queries, query_maps, keys, values, kwin, vwin, far, bias)


def scatter_kernel(src, out, own_sem, send, recv):
    z, x, y, h, c = here()
    me = h * 2 + c
    rows = BLOCK // 4

    def peer(o):
        j = lax.rem(me + o, 4)
        return j, (z, x, y, j // 2, lax.rem(j, 2))

    barrier = pltpu.get_barrier_semaphore()
    for o in range(1, 4):
        pl.semaphore_signal(barrier, inc=1, device_id=peer(o)[1], device_id_type=MESH)
    pl.semaphore_wait(barrier, 3)

    def columns(j):
        return pl.ds(pl.multiple_of(j * QL, QL), QL)

    def copy_to(o):
        j, device = peer(o)
        piece = src.at[:, pl.ds(pl.multiple_of(j * rows, rows), rows), :]
        return remote(piece, out.at[:, :, columns(me)], send.at[o], recv.at[me], device)

    for o in (2, 1, 3):
        copy_to(o).start()
    mine = pltpu.make_async_copy(
        src.at[:, pl.ds(pl.multiple_of(me * rows, rows), rows), :], out.at[:, :, columns(me)], own_sem.at[0]
    )
    mine.start()
    mine.wait()
    for o in range(1, 4):
        copy_to(o).wait_send()
        j = lax.rem(me - o + 4, 4)
        remote(out.at[:, :, columns(j)], out.at[:, :, columns(j)], send.at[o], recv.at[j], peer(o)[1]).wait_recv()


def scatter(attended):
    dma = pltpu.SemaphoreType.DMA
    return pl.pallas_call(
        scatter_kernel,
        out_shape=jax.ShapeDtypeStruct((SEQS, BLOCK // 4, 4 * QL), F32),
        in_specs=[pl.BlockSpec(memory_space=pltpu.VMEM)],
        out_specs=pl.BlockSpec(memory_space=pltpu.VMEM),
        scratch_shapes=[dma((1,)), dma((4,)), dma((4,))],
        name="scatter",
        compiler_params=pltpu.CompilerParams(collective_id=1, has_side_effects=True),
    )(attended)


def on_device(queries, keys, values, query_maps, key_maps, mix, window_blocks, starts):
    ctx = lax.axis_index(CTX)
    anchor = ctx * BLOCK
    place = lax.rem(ctx, PLANE)
    rows = jnp.arange(BLOCK, dtype=jnp.int32)
    prev_live = ((anchor - PLANE * BLOCK + rows)[None, :] >= starts[:, None]) & ((anchor - PLANE * BLOCK) >= 0)
    mask = jnp.broadcast_to(prev_live[:, :, None], (SEQS, BLOCK, HD)).astype(F32)
    col = jnp.arange(WIN, dtype=jnp.int32)
    slot = col // BLOCK
    distance = jnp.where(slot < place, place - slot, place - slot + PLANE)
    picked = (window_blocks >> jnp.maximum(distance - 1, 0)[None, :]) & 1
    position = anchor - distance * BLOCK + lax.rem(col, BLOCK)
    earlier = (picked == 1) & (position >= 0) & (position >= starts[:, None])
    own = (anchor + col - PLANE * BLOCK) >= starts[:, None]
    allowed = jnp.where(slot < PLANE, earlier, jnp.where(slot == PLANE, own, False))
    bias = jnp.where(allowed, 0.0, NEG).astype(F32)
    bias = jnp.broadcast_to(bias[:, None, :], (SEQS, 8, WIN))
    info = jnp.concatenate([starts, anchor[None]]).astype(jnp.int32)
    weight = jax.nn.sigmoid(mix)
    kwin, vwin, far = gather(keys, values, key_maps, mask)
    attended = attend(info, weight, queries, query_maps, keys, values, kwin, vwin, far, bias)
    return scatter(attended)


def solution(mesh):
    torus = Mesh(mesh.devices.reshape(8, 2, 4, 2, 2), ("ctx_0", "ctx_1", "ctx_2", "kv_0", "kv_1"))
    in_specs = (
        P(None, CTX, KV),
        P(None, CTX, KV),
        P(None, CTX, KV),
        P(KV, None, None),
        P(KV, None, None),
        P(KV),
        P(None, CTX),
        P(),
    )
    out_specs = P(None, CTX_KV, None)
    return jax.shard_map(
        on_device, mesh=torus, in_specs=in_specs, out_specs=out_specs, check_vma=False
    )
```

```python
import functools

import jax
import jax.numpy as jnp
from jax import lax
from jax.experimental import pallas as pl
from jax.experimental.pallas import tpu as pltpu
from jax.sharding import Mesh
from jax.sharding import PartitionSpec as P

HD = 128
HALF = 128
FEAT = 2 * HALF
BLOCK = 64
WBLK = 8
GROUP = 16
PLANE = 8
PLANES = 8
SEQS = 2
KVL = 2
COMBOS = SEQS * KVL
QL = KVL * GROUP * HD
WIN = 640
PIECE = 24
HEADS = 4
ROWS = BLOCK // 4
NEG = -1e30
CTX = ("ctx_0", "ctx_1", "ctx_2")
KV = ("kv_0", "kv_1")
CTX_KV = CTX + KV
MESH = pl.DeviceIdType.MESH
F32 = jnp.float32
BF16 = jnp.bfloat16
HIGHEST = lax.Precision.HIGHEST

NN = (((1,), (0,)), ((), ()))
NT = (((1,), (1,)), ((), ()))
TN = (((0,), (0,)), ((), ()))


def remote(src, dst, send, recv, device):
    return pltpu.make_async_remote_copy(
        src_ref=src, dst_ref=dst, send_sem=send, recv_sem=recv, device_id=device, device_id_type=MESH
    )


def mm(a, b, dims):
    return lax.dot_general(a, b, dims, preferred_element_type=F32)


def split(x):
    hi = x.astype(BF16)
    return hi, (x - hi.astype(F32)).astype(BF16)


def softmax_pair(logits):
    up = jnp.exp(logits)
    down = jnp.exp(-logits)
    up = up / jnp.sum(up, axis=-1, keepdims=True)
    down = down / jnp.sum(down, axis=-1, keepdims=True)
    return jnp.concatenate([up, down], axis=-1)


def here():
    return [lax.axis_index(a) for a in CTX_KV]


def features(x, weights):
    x_hi, x_lo = split(x)
    w_hi, w_lo = split(weights)
    w = jnp.concatenate([w_hi, w_lo], axis=1)
    both = mm(jnp.concatenate([x_hi, x_lo], axis=1), jnp.concatenate([w, w], axis=0), NN)
    return both[:, :HALF] + both[:, HALF:]


def kernel(
    starts_ref, bits_ref, mix_ref, q_hbm, k_hbm, v_hbm, qm_hbm, km_hbm, out,
    q, qm, km, own, prev, kvw, a_tx, a_rx, t_tx, t_rx, d_tx, far, p_hi, p_lo, near, mine,
    k_hi, k_lo, v_hi, v_lo, f_hi, f_lo,
    ld_own, ld_q, ld_qm, ld_km, z_send, z_recv, w_send, w_recv,
    a_send, a_recv, t_send, t_recv, d_send, d_recv, o_send, o_recv, o_own,
):
    z, x, y, h, c = here()
    me = x * 4 + y
    kv = h * 2 + c
    anchor = (z * PLANE + me) * BLOCK

    def lanes(n):
        return slice((n % KVL) * HD, (n % KVL + 1) * HD)

    def plane(o):
        j = lax.rem(me + o, PLANE)
        return j, (z, j // 4, lax.rem(j, 4), h, c)

    def column(o):
        j = lax.rem(z + o, PLANES)
        return j, (j, x, y, h, c)

    def line(o):
        j = lax.rem(y + o, 4)
        return j, (z, x, j, h, c)

    def ring(o):
        j = lax.rem(kv + o, 4)
        return j, (z, x, y, j // 2, lax.rem(j, 2))

    partner = (z, 1 - x, y, h, c)

    loads_own = {}
    for n in range(COMBOS):
        for t, hbm in enumerate((k_hbm, v_hbm)):
            loads_own[n, t] = pltpu.make_async_copy(hbm.at[n // KVL, :, lanes(n)], own.at[n, t], ld_own.at[n, t])
            loads_own[n, t].start()
    load_km = pltpu.make_async_copy(km_hbm, km, ld_km.at[0])
    load_km.start()
    loads_qm = []
    loads_q = []
    for g in range(KVL):
        loads_qm.append(
            pltpu.make_async_copy(qm_hbm.at[g * GROUP:(g + 1) * GROUP], qm.at[g * GROUP:(g + 1) * GROUP], ld_qm.at[g])
        )
    for n in range(COMBOS):
        g = n % KVL
        loads_q.append(
            pltpu.make_async_copy(q_hbm.at[n // KVL, :, g * GROUP * HD:(g + 1) * GROUP * HD], q.at[n], ld_q.at[n])
        )
    for copy in (loads_q[0], loads_qm[0], loads_q[1], loads_qm[1], loads_q[2], loads_q[3]):
        copy.start()

    barrier = pltpu.get_barrier_semaphore()
    greeted = [plane(o)[1] for o in range(1, PLANE)] + [column(o)[1] for o in range(1, PLANES)]
    greeted += [ring(o)[1] for o in range(1, 4)]
    for device in greeted:
        pl.semaphore_signal(barrier, inc=1, device_id=device, device_id_type=MESH)
    pl.semaphore_wait(barrier, len(greeted))

    def shift(n):
        return remote(own.at[n], prev.at[n], z_send.at[n], z_recv.at[n], column(1)[1])

    def to_line(n, o, source):
        return remote(source.at[n], kvw.at[n, me], w_send.at[n, o], w_recv.at[n, me], line(o)[1])

    def to_partner(n, source):
        return remote(source.at[n], kvw.at[n, me], w_send.at[n, 0], w_recv.at[n, me], partner)

    other = (1 - x) * 4 + y

    def forward(n, o):
        return remote(kvw.at[n, other], kvw.at[n, other], w_send.at[n, 3 + o], w_recv.at[n, other], line(o)[1])

    def window_own(n):
        @pl.when(x == 0)
        def _():
            to_partner(n, own).start()

        for o in range(1, 4):
            @pl.when(y + o < 4)
            def _():
                to_line(n, o, own).start()

    def window_prev(n):
        @pl.when(x == 1)
        def _():
            to_partner(n, prev).start()

        for o in range(1, 4):
            @pl.when(y + o >= 4)
            def _():
                to_line(n, o, prev).start()

        kvw[n, me] = prev[n]

    def arrived(n, slot):
        return remote(kvw.at[n, slot], kvw.at[n, slot], w_send.at[n, 0], w_recv.at[n, slot], partner)

    def window_forward(n):
        arrived(n, other).wait_recv()
        for o in range(1, 4):
            forward(n, o).start()

    def to_owner(n, o):
        j, device = plane(o)
        return remote(a_tx.at[n, j], a_rx.at[n, me], a_send.at[n, o], a_recv.at[n, me], device)

    def state(n):
        s, g = n // KVL, n % KVL
        shift(n).wait_recv()
        phi = softmax_pair(features(prev[n, 0], km[g]))
        row = lax.broadcasted_iota(jnp.int32, (BLOCK, FEAT), 0)
        position = row + (anchor - PLANE * BLOCK)
        phi = jnp.where((position >= 0) & (position >= starts_ref[s]), phi, 0.0)
        hi, lo = split(phi)
        v_h, v_l = split(prev[n, 1])
        total = mm(jnp.concatenate([v_h, v_l], axis=0), jnp.concatenate([hi, hi], axis=0), TN) + mm(v_h, lo, TN)
        norm = jnp.broadcast_to(jnp.sum(phi, axis=0, keepdims=True), (8, FEAT))
        for j in range(PLANE):
            a_tx[n, j, 0:16, :] = total[j * 16:(j + 1) * 16]
            a_tx[n, j, 16:24, :] = norm
        for o in range(1, PLANE):
            to_owner(n, o).start()
        a_rx[n, me] = a_tx[n, me]

    def from_plane(n, o, buf, send, recv):
        j = lax.rem(me - o + PLANE, PLANE)
        return remote(buf.at[n, j], buf.at[n, j], send.at[n, o], recv.at[n, j], plane(o)[1])

    def to_later(n, o):
        return remote(t_tx.at[n], t_rx.at[n, z], t_send.at[n, o], t_recv.at[n, z], column(o)[1])

    def owner_total(n):
        for o in range(1, PLANE):
            from_plane(n, o, a_rx, a_send, a_recv).wait_recv()
        total = a_rx[n, 0]
        for j in range(1, PLANE):
            total = total + a_rx[n, j]
        t_tx[n] = total
        for o in range(1, PLANES):
            @pl.when(z + o < PLANES)
            def _():
                to_later(n, o).start()

    def to_reader(n, o):
        j, device = plane(o)
        return remote(d_tx.at[n, j], far.at[n, me], d_send.at[n, o], d_recv.at[n, me], device)

    def owner_prefix(n):
        d_tx[n, 0] = jnp.zeros((PIECE, FEAT), F32)
        for j in range(PLANES - 1):
            @pl.when(j < z)
            def _():
                remote(t_tx.at[n], t_rx.at[n, j], t_send.at[n, 1], t_recv.at[n, j], partner).wait_recv()
                d_tx[n, 0] = d_tx[n, 0] + t_rx[n, j]
        running = d_tx[n, 0]
        for j in range(PLANE - 1):
            running = running + a_rx[n, j]
            d_tx[n, j + 1] = running
        for o in range(1, PLANE):
            to_reader(n, o).start()
        far[n, me] = d_tx[n, me]

    def query_features(n):
        g = n % KVL
        loads_q[n].wait()
        if n < KVL:
            loads_qm[g].wait()

        @pl.loop(0, GROUP // HEADS)
        def _(step):
            wide = q[n, :, pl.ds(pl.multiple_of(step * HEADS * HD, HEADS * HD), HEADS * HD)]
            logits = []
            for k in range(HEADS):
                logits.append(features(wide[:, k * HD:(k + 1) * HD], qm[g * GROUP + step * HEADS + k]))
            hi, lo = split(softmax_pair(jnp.concatenate(logits, axis=0)))
            place = pl.ds(pl.multiple_of(step * HEADS * BLOCK, HEADS * BLOCK), HEADS * BLOCK)
            p_hi[n, place, :] = hi
            p_lo[n, place, :] = lo

    def attend_near(n):
        s = n // KVL
        for o in range(1, 4):
            j = line(o)[0]
            arrived(n, x * 4 + j).wait_recv()
            arrived(n, (1 - x) * 4 + j).wait_recv()
        zeros = jnp.zeros((WIN - (WBLK + 1) * BLOCK, HD), F32)
        hi, lo = split(jnp.concatenate([kvw[n, j, 0] for j in range(PLANE)] + [own[n, 0], zeros], axis=0))
        k_hi[...] = jnp.concatenate([hi, hi], axis=1)
        k_lo[...] = jnp.concatenate([lo, lo], axis=1)
        hi, lo = split(jnp.concatenate([kvw[n, j, 1] for j in range(PLANE)] + [own[n, 1], zeros], axis=0))
        v_hi[...] = jnp.concatenate([hi, jnp.ones((WIN, HD), BF16)], axis=1)
        v_lo[...] = lo
        start = starts_ref[s]
        column_id = lax.broadcasted_iota(jnp.int32, (8, WIN), 1)
        slot = column_id // BLOCK
        distance = jnp.where(slot < me, me - slot, me - slot + PLANE)
        bits = jnp.broadcast_to(bits_ref[s, 0], (8, WIN))
        picked = lax.shift_right_logical(bits, jnp.maximum(distance - 1, 0)) & 1
        position = anchor - distance * BLOCK + (column_id & (BLOCK - 1))
        earlier = (slot < PLANE) & (picked == 1) & (position >= 0) & (position >= start)
        bias = jnp.where(earlier, 0.0, NEG)[:1, :WBLK * BLOCK]
        row = lax.broadcasted_iota(jnp.int32, (HEADS * BLOCK, HD), 0) & (BLOCK - 1)
        col = lax.broadcasted_iota(jnp.int32, (HEADS * BLOCK, HD), 1)
        own_bias = jnp.where((col <= row) & (anchor + col >= start), 0.0, NEG)

        @pl.loop(0, GROUP // HEADS)
        def _(step):
            wide = q[n, :, pl.ds(pl.multiple_of(step * HEADS * HD, HEADS * HD), HEADS * HD)]
            rows = jnp.concatenate([wide[:, k * HD:(k + 1) * HD] for k in range(HEADS)], axis=0)
            q_hi, q_lo = split(rows * HD ** -0.5)
            both = jnp.concatenate([q_hi, q_lo], axis=1)
            scores = mm(both, k_hi[...], NT) + mm(both, k_lo[...], NT)
            scores = jnp.concatenate(
                [scores[:, :WBLK * BLOCK] + bias, scores[:, WBLK * BLOCK:] + own_bias], axis=1
            )
            top = jnp.max(scores, axis=1, keepdims=True)
            e_hi, e_lo = split(jnp.exp(scores - top))
            wide_sum = mm(e_hi, v_hi[...], NN) + mm(e_lo, v_hi[...], NN)
            extra = mm(e_hi, v_lo[...], NN)
            place = pl.ds(pl.multiple_of(step * HEADS * BLOCK, HEADS * BLOCK), HEADS * BLOCK)
            near[n, place, :] = jnp.concatenate([wide_sum[:, :HD] + extra, wide_sum[:, HD:]], axis=1)

    def to_keeper(n, o):
        s, g = n // KVL, n % KVL
        j, device = ring(o)
        piece = mine.at[n, pl.ds(pl.multiple_of(j * ROWS, ROWS), ROWS), :]
        return remote(piece, out.at[s, :, columns(g, kv)], o_send.at[n, o], o_recv.at[n, kv], device)

    def columns(g, j):
        return pl.ds(pl.multiple_of(j * QL + g * GROUP * HD, GROUP * HD), GROUP * HD)

    def to_self(n):
        s, g = n // KVL, n % KVL
        piece = mine.at[n, pl.ds(pl.multiple_of(kv * ROWS, ROWS), ROWS), :]
        return pltpu.make_async_copy(piece, out.at[s, :, columns(g, kv)], o_own.at[n])

    def finish(n):
        s, g = n // KVL, n % KVL
        for o in range(1, PLANE):
            from_plane(n, o, far, d_send, d_recv).wait_recv()
        total = jnp.concatenate([far[n, j, 0:16, :] for j in range(PLANE)], axis=0)
        norm = jnp.broadcast_to(far[n, 0, 16:17, :], (HD, FEAT))
        hi, lo = split(jnp.concatenate([total, norm], axis=0))
        f_hi[...] = hi
        f_lo[...] = lo
        row = lax.broadcasted_iota(jnp.int32, (BLOCK, HD), 0)
        live = (row + anchor) >= starts_ref[s]

        @pl.loop(0, GROUP // HEADS)
        def _(step):
            place = pl.ds(pl.multiple_of(step * HEADS * BLOCK, HEADS * BLOCK), HEADS * BLOCK)
            hi = p_hi[n, place, :]
            distant = mm(hi, f_hi[...], NT) + mm(p_lo[n, place, :], f_hi[...], NT) + mm(hi, f_lo[...], NT)
            close = near[n, place, :]
            for k in range(HEADS):
                head = step * HEADS + k
                a = jax.nn.sigmoid(jnp.full((1, HD), mix_ref[g * GROUP + head], F32))
                part = slice(k * BLOCK, (k + 1) * BLOCK)
                top_part = a * close[part, :HD] + (1.0 - a) * distant[part, :HD]
                bottom = a * close[part, HD:] + (1.0 - a) * distant[part, HD:]
                result = jnp.where(live, top_part / jnp.where(live, bottom, 1.0), 0.0)
                mine[n, :, pl.ds(pl.multiple_of(head * HD, HD), HD)] = result

        for o in (2, 1, 3):
            to_keeper(n, o).start()
        to_self(n).start()

    for n in range(COMBOS):
        for t in range(2):
            loads_own[n, t].wait()
        shift(n).start()
    window_own(0)
    load_km.wait()
    query_features(0)
    for n in range(COMBOS):
        state(n)
        window_prev(n)
        if n + 1 < COMBOS:
            window_own(n + 1)
        if n > 0:
            window_forward(n - 1)
    owner_total(0)
    window_forward(COMBOS - 1)
    for n in range(1, COMBOS):
        query_features(n)
        owner_total(n)
    attend_near(0)
    owner_prefix(0)
    owner_prefix(1)
    attend_near(1)
    owner_prefix(2)
    owner_prefix(3)
    finish(0)
    attend_near(2)
    finish(1)
    attend_near(3)
    finish(2)
    finish(3)

    for n in range(COMBOS):
        shift(n).wait_send()
        to_partner(n, own).wait_send()
        for o in range(1, 4):
            to_line(n, o, own).wait_send()
            forward(n, o).wait_send()
        for o in range(1, PLANE):
            to_owner(n, o).wait_send()
            to_reader(n, o).wait_send()
        for o in range(1, PLANES):
            @pl.when(z + o < PLANES)
            def _():
                to_later(n, o).wait_send()
    for n in range(COMBOS):
        s, g = n // KVL, n % KVL
        to_self(n).wait()
        for o in range(1, 4):
            to_keeper(n, o).wait_send()
            j = lax.rem(kv - o + 4, 4)
            landed = out.at[s, :, columns(g, j)]
            remote(landed, landed, o_send.at[n, o], o_recv.at[n, j], ring(o)[1]).wait_recv()


def on_device(queries, keys, values, query_maps, key_maps, mix, window_blocks, starts):
    smem = pl.BlockSpec(memory_space=pltpu.SMEM)
    hbm = pl.BlockSpec(memory_space=pl.ANY)
    dma = pltpu.SemaphoreType.DMA
    vmem = pltpu.VMEM
    pieces = (COMBOS, PLANE, PIECE, FEAT)
    return pl.pallas_call(
        kernel,
        out_shape=jax.ShapeDtypeStruct((SEQS, ROWS, 4 * QL), F32),
        in_specs=[smem, smem, smem] + [hbm] * 5,
        out_specs=hbm,
        scratch_shapes=[
            vmem((COMBOS, BLOCK, GROUP * HD), F32),
            vmem((KVL * GROUP, HD, HALF), F32),
            vmem((KVL, HD, HALF), F32),
            vmem((COMBOS, 2, BLOCK, HD), F32),
            vmem((COMBOS, 2, BLOCK, HD), F32),
            vmem((COMBOS, PLANE, 2, BLOCK, HD), F32),
            vmem(pieces, F32),
            vmem(pieces, F32),
            vmem((COMBOS, PIECE, FEAT), F32),
            vmem(pieces, F32),
            vmem(pieces, F32),
            vmem(pieces, F32),
            vmem((COMBOS, GROUP * BLOCK, FEAT), BF16),
            vmem((COMBOS, GROUP * BLOCK, FEAT), BF16),
            vmem((COMBOS, GROUP * BLOCK, 2 * HD), F32),
            vmem((COMBOS, BLOCK, GROUP * HD), F32),
            vmem((WIN, 2 * HD), BF16),
            vmem((WIN, 2 * HD), BF16),
            vmem((WIN, 2 * HD), BF16),
            vmem((WIN, HD), BF16),
            vmem((2 * HD, FEAT), BF16),
            vmem((2 * HD, FEAT), BF16),
            dma((COMBOS, 2)), dma((COMBOS,)), dma((KVL,)), dma((1,)), dma((COMBOS,)), dma((COMBOS,)),
            dma((COMBOS, 7)), dma((COMBOS, 8)),
            dma((COMBOS, 8)), dma((COMBOS, 8)), dma((COMBOS, 8)), dma((COMBOS, 8)), dma((COMBOS, 8)), dma((COMBOS, 8)),
            dma((COMBOS, 4)), dma((COMBOS, 4)), dma((COMBOS,)),
        ],
        name="hybrid",
        compiler_params=pltpu.CompilerParams(
            collective_id=0, has_side_effects=True, vmem_limit_bytes=62 << 20
        ),
    )(starts, window_blocks, mix, queries, keys, values, query_maps, key_maps)


def solution(mesh):
    torus = Mesh(mesh.devices.reshape(8, 2, 4, 2, 2), ("ctx_0", "ctx_1", "ctx_2", "kv_0", "kv_1"))
    in_specs = (
        P(None, CTX, KV),
        P(None, CTX, KV),
        P(None, CTX, KV),
        P(KV, None, None),
        P(KV, None, None),
        P(KV),
        P(None, CTX),
        P(),
    )
    out_specs = P(None, CTX_KV, None)
    return jax.shard_map(
        on_device, mesh=torus, in_specs=in_specs, out_specs=out_specs, check_vma=False
    )
```

```python
import functools

import jax
import jax.numpy as jnp
from jax import lax
from jax.experimental import pallas as pl
from jax.experimental.pallas import tpu as pltpu
from jax.sharding import Mesh
from jax.sharding import PartitionSpec as P

HD = 128
HALF = 128
FEAT = 2 * HALF
BLOCK = 64
WBLK = 8
GROUP = 16
PLANE = 8
PLANES = 8
SEQS = 2
KVL = 2
COMBOS = SEQS * KVL
QL = KVL * GROUP * HD
WIN = 640
PIECE = 16
HEADS = 4
STEPS = GROUP // HEADS
ROWS = BLOCK // 4
NEG = -1e30
CTX = ("ctx_0", "ctx_1", "ctx_2")
KV = ("kv_0", "kv_1")
CTX_KV = CTX + KV
MESH = pl.DeviceIdType.MESH
F32 = jnp.float32
BF16 = jnp.bfloat16
HIGHEST = lax.Precision.HIGHEST

NN = (((1,), (0,)), ((), ()))
NT = (((1,), (1,)), ((), ()))
TN = (((0,), (0,)), ((), ()))


def remote(src, dst, send, recv, device):
    return pltpu.make_async_remote_copy(
        src_ref=src, dst_ref=dst, send_sem=send, recv_sem=recv, device_id=device, device_id_type=MESH
    )


def mm(a, b, dims):
    return lax.dot_general(a, b, dims, preferred_element_type=F32)


def split(x):
    hi = x.astype(BF16)
    return hi, (x - hi.astype(F32)).astype(BF16)


def softmax_pair(logits):
    up = jnp.exp(logits)
    down = jnp.exp(-logits)
    up = up / jnp.sum(up, axis=-1, keepdims=True)
    down = down / jnp.sum(down, axis=-1, keepdims=True)
    return jnp.concatenate([up, down], axis=-1)


def here():
    return [lax.axis_index(a) for a in CTX_KV]


def features(x, weights):
    x_hi, x_lo = split(x)
    w_hi, w_lo = split(weights)
    w = jnp.concatenate([w_hi, w_lo], axis=1)
    both = mm(jnp.concatenate([x_hi, x_lo], axis=1), jnp.concatenate([w, w], axis=0), NN)
    return both[:, :HALF] + both[:, HALF:]


def kernel(
    starts_ref, bits_ref, mix_ref, q_hbm, k_hbm, v_hbm, qm_hbm, km_hbm, out,
    q, qm, km, own, prev, kvw, a_tx, a_rx, t_tx, t_rx, d_tx, far, p_hi, p_lo, near, mine,
    k_hi, k_lo, v_hi, v_lo, f_hi, f_lo, n_tx, n_rx, m_tx, m_rx, norms,
    ld_own, ld_q, ld_qm, ld_km, z_send, z_recv, w_send, w_recv,
    a_send, a_recv, t_send, t_recv, d_send, d_recv, o_send, o_recv, o_own,
    n_send, n_recv, m_send, m_recv,
):
    z, x, y, h, c = here()
    me = x * 4 + y
    kv = h * 2 + c
    anchor = (z * PLANE + me) * BLOCK

    def lanes(n):
        return slice((n % KVL) * HD, (n % KVL + 1) * HD)

    def plane(o):
        j = lax.rem(me + o, PLANE)
        return j, (z, j // 4, lax.rem(j, 4), h, c)

    def column(o):
        j = lax.rem(z + o, PLANES)
        return j, (j, x, y, h, c)

    def line(o):
        j = lax.rem(y + o, 4)
        return j, (z, x, j, h, c)

    def ring(o):
        j = lax.rem(kv + o, 4)
        return j, (z, x, y, j // 2, lax.rem(j, 2))

    partner = (z, 1 - x, y, h, c)

    loads_own = {}
    for n in range(COMBOS):
        for t, hbm in enumerate((k_hbm, v_hbm)):
            loads_own[n, t] = pltpu.make_async_copy(hbm.at[n // KVL, :, lanes(n)], own.at[n, t], ld_own.at[n, t])
            loads_own[n, t].start()
    load_km = pltpu.make_async_copy(km_hbm, km, ld_km.at[0])
    load_km.start()
    loads_qm = []
    loads_q = []
    for g in range(KVL):
        loads_qm.append(
            pltpu.make_async_copy(qm_hbm.at[g * GROUP:(g + 1) * GROUP], qm.at[g * GROUP:(g + 1) * GROUP], ld_qm.at[g])
        )
    for n in range(COMBOS):
        g = n % KVL
        loads_q.append(
            pltpu.make_async_copy(q_hbm.at[n // KVL, :, g * GROUP * HD:(g + 1) * GROUP * HD], q.at[n], ld_q.at[n])
        )
    for copy in (loads_q[0], loads_qm[0], loads_q[1], loads_qm[1], loads_q[2], loads_q[3]):
        copy.start()

    barrier = pltpu.get_barrier_semaphore()
    greeted = [plane(o)[1] for o in range(1, PLANE)] + [column(o)[1] for o in range(1, PLANES)]
    greeted += [ring(o)[1] for o in range(1, 4)]
    for device in greeted:
        pl.semaphore_signal(barrier, inc=1, device_id=device, device_id_type=MESH)
    pl.semaphore_wait(barrier, len(greeted))

    def shift(n):
        return remote(own.at[n], prev.at[n], z_send.at[n], z_recv.at[n], column(1)[1])

    def to_line(n, o, source):
        return remote(source.at[n], kvw.at[n, me], w_send.at[n, o], w_recv.at[n, me], line(o)[1])

    def to_partner(n, source):
        return remote(source.at[n], kvw.at[n, me], w_send.at[n, 0], w_recv.at[n, me], partner)

    other = (1 - x) * 4 + y

    def forward(n, o):
        return remote(kvw.at[n, other], kvw.at[n, other], w_send.at[n, 3 + o], w_recv.at[n, other], line(o)[1])

    def window_own(n):
        @pl.when(x == 0)
        def _():
            to_partner(n, own).start()

        for o in (1, 3):
            @pl.when(y + o < 4)
            def _():
                to_line(n, o, own).start()

    def window_prev(n):
        @pl.when(x == 1)
        def _():
            to_partner(n, prev).start()

        for o in (1, 3):
            @pl.when(y + o >= 4)
            def _():
                to_line(n, o, prev).start()

        kvw[n, me] = prev[n]

    def arrived(n, slot):
        return remote(kvw.at[n, slot], kvw.at[n, slot], w_send.at[n, 0], w_recv.at[n, slot], partner)

    def window_forward(n):
        arrived(n, other).wait_recv()
        for o in (1, 3):
            forward(n, o).start()

    swing = 1 - 2 * lax.rem(y, 2)
    ahead = lax.rem(y + swing + 4, 4)
    behind = lax.rem(y - swing + 4, 4)

    def relay(n, slot, k, to):
        return remote(kvw.at[n, slot], kvw.at[n, slot], w_send.at[n, k], w_recv.at[n, slot], (z, x, to, h, c))

    def relay_same(n):
        return relay(n, x * 4 + behind, 2, ahead)

    def relay_other(n):
        return relay(n, (1 - x) * 4 + ahead, 5, behind)

    def window_relay(n):
        arrived(n, x * 4 + behind).wait_recv()
        relay_same(n).start()
        arrived(n, (1 - x) * 4 + ahead).wait_recv()
        relay_other(n).start()

    def to_owner(n, o):
        j, device = plane(o)
        return remote(a_tx.at[n, j], a_rx.at[n, me], a_send.at[n, o], a_recv.at[n, me], device)

    def state(n):
        s, g = n // KVL, n % KVL
        shift(n).wait_recv()
        phi = softmax_pair(features(prev[n, 0], km[g]))
        row = lax.broadcasted_iota(jnp.int32, (BLOCK, FEAT), 0)
        position = row + (anchor - PLANE * BLOCK)
        phi = jnp.where((position >= 0) & (position >= starts_ref[s]), phi, 0.0)
        hi, lo = split(phi)
        v_h, v_l = split(prev[n, 1])
        total = mm(jnp.concatenate([v_h, v_l], axis=0), jnp.concatenate([hi, hi], axis=0), TN) + mm(v_h, lo, TN)
        for j in range(PLANE):
            a_tx[n, j] = total[j * PIECE:(j + 1) * PIECE]
        n_tx[n:n + 1, :] = jnp.sum(phi, axis=0, keepdims=True)
        for o in range(1, PLANE):
            to_owner(n, o).start()
        a_rx[n, me] = a_tx[n, me]

    def norm_to_plane(o):
        return remote(n_tx, n_rx.at[me], n_send.at[o], n_recv.at[me], plane(o)[1])

    def norm_to_later(o):
        return remote(m_tx, m_rx.at[z], m_send.at[o], m_recv.at[z], column(o)[1])

    def norm_start():
        for o in range(1, PLANE):
            norm_to_plane(o).start()
        n_rx[me] = n_tx[...]

    def norm_total():
        for o in range(1, PLANE):
            j = lax.rem(me - o + PLANE, PLANE)
            remote(n_rx.at[j], n_rx.at[j], n_send.at[o], n_recv.at[j], plane(o)[1]).wait_recv()
        total = jnp.zeros((8, FEAT), F32)
        inside = jnp.zeros((8, FEAT), F32)
        for j in range(PLANE):
            total = total + n_rx[j]
            inside = jnp.where(j < me, total, inside)
        m_tx[...] = total
        norms[...] = inside
        for o in range(1, PLANES):
            @pl.when(z + o < PLANES)
            def _():
                norm_to_later(o).start()

    def norm_finish():
        for j in range(PLANES - 1):
            @pl.when(j < z)
            def _():
                remote(m_tx, m_rx.at[j], m_send.at[1], m_recv.at[j], partner).wait_recv()
                norms[...] = norms[...] + m_rx[j]

    def from_plane(n, o, buf, send, recv):
        j = lax.rem(me - o + PLANE, PLANE)
        return remote(buf.at[n, j], buf.at[n, j], send.at[n, o], recv.at[n, j], plane(o)[1])

    def to_later(n, o):
        return remote(t_tx.at[n], t_rx.at[n, z], t_send.at[n, o], t_recv.at[n, z], column(o)[1])

    def owner_total(n):
        for o in range(1, PLANE):
            from_plane(n, o, a_rx, a_send, a_recv).wait_recv()
        total = a_rx[n, 0]
        for j in range(1, PLANE):
            total = total + a_rx[n, j]
        t_tx[n] = total
        for o in range(1, PLANES):
            @pl.when(z + o < PLANES)
            def _():
                to_later(n, o).start()

    def to_reader(n, o):
        j, device = plane(o)
        return remote(d_tx.at[n, j], far.at[n, me], d_send.at[n, o], d_recv.at[n, me], device)

    def owner_prefix(n):
        d_tx[n, 0] = jnp.zeros((PIECE, FEAT), F32)
        for j in range(PLANES - 1):
            @pl.when(j < z)
            def _():
                remote(t_tx.at[n], t_rx.at[n, j], t_send.at[n, 1], t_recv.at[n, j], partner).wait_recv()
                d_tx[n, 0] = d_tx[n, 0] + t_rx[n, j]
        running = d_tx[n, 0]
        for j in range(PLANE - 1):
            running = running + a_rx[n, j]
            d_tx[n, j + 1] = running
        for o in range(1, PLANE):
            to_reader(n, o).start()
        far[n, me] = d_tx[n, me]

    def query_features(n):
        g = n % KVL
        loads_q[n].wait()
        if n < KVL:
            loads_qm[g].wait()

        @pl.loop(0, STEPS)
        def _(step):
            wide = q[n, :, pl.ds(pl.multiple_of(step * HEADS * HD, HEADS * HD), HEADS * HD)]
            logits = []
            for k in range(HEADS):
                logits.append(features(wide[:, k * HD:(k + 1) * HD], qm[g * GROUP + step * HEADS + k]))
            hi, lo = split(softmax_pair(jnp.concatenate(logits, axis=0)))
            place = pl.ds(pl.multiple_of(step * HEADS * BLOCK, HEADS * BLOCK), HEADS * BLOCK)
            p_hi[n, place, :] = hi
            p_lo[n, place, :] = lo

    def attend_near(n):
        s = n // KVL
        opposite = line(2)[0]
        for slot in (x * 4 + ahead, x * 4 + opposite, (1 - x) * 4 + behind, (1 - x) * 4 + opposite):
            arrived(n, slot).wait_recv()
        zeros = jnp.zeros((WIN - (WBLK + 1) * BLOCK, HD), F32)
        hi, lo = split(jnp.concatenate([kvw[n, j, 0] for j in range(PLANE)] + [own[n, 0], zeros], axis=0))
        k_hi[...] = jnp.concatenate([hi, hi], axis=1)
        k_lo[...] = jnp.concatenate([lo, lo], axis=1)
        hi, lo = split(jnp.concatenate([kvw[n, j, 1] for j in range(PLANE)] + [own[n, 1], zeros], axis=0))
        v_hi[...] = jnp.concatenate([hi, jnp.ones((WIN, HD), BF16)], axis=1)
        v_lo[...] = lo
        start = starts_ref[s]
        column_id = lax.broadcasted_iota(jnp.int32, (8, WIN), 1)
        slot = column_id // BLOCK
        distance = jnp.where(slot < me, me - slot, me - slot + PLANE)
        bits = jnp.broadcast_to(bits_ref[0, s], (8, WIN))
        picked = lax.shift_right_logical(bits, jnp.maximum(distance - 1, 0)) & 1
        position = anchor - distance * BLOCK + (column_id & (BLOCK - 1))
        earlier = (slot < PLANE) & (picked == 1) & (position >= 0) & (position >= start)
        bias = jnp.where(earlier, 0.0, NEG)[:1, :WBLK * BLOCK]
        row = lax.broadcasted_iota(jnp.int32, (HEADS * BLOCK, HD), 0) & (BLOCK - 1)
        col = lax.broadcasted_iota(jnp.int32, (HEADS * BLOCK, HD), 1)
        own_bias = jnp.where((col <= row) & (anchor + col >= start), 0.0, NEG)

        @pl.loop(0, STEPS)
        def _(step):
            wide = q[n, :, pl.ds(pl.multiple_of(step * HEADS * HD, HEADS * HD), HEADS * HD)]
            rows = jnp.concatenate([wide[:, k * HD:(k + 1) * HD] for k in range(HEADS)], axis=0)
            q_hi, q_lo = split(rows * HD ** -0.5)
            both = jnp.concatenate([q_hi, q_lo], axis=1)
            scores = mm(both, k_hi[...], NT) + mm(both, k_lo[...], NT)
            scores = jnp.concatenate(
                [scores[:, :WBLK * BLOCK] + bias, scores[:, WBLK * BLOCK:] + own_bias], axis=1
            )
            top = jnp.max(scores, axis=1, keepdims=True)
            e_hi, e_lo = split(jnp.exp(scores - top))
            wide_sum = mm(e_hi, v_hi[...], NN) + mm(e_lo, v_hi[...], NN)
            extra = mm(e_hi, v_lo[...], NN)
            place = pl.ds(pl.multiple_of(step * HEADS * BLOCK, HEADS * BLOCK), HEADS * BLOCK)
            near[n, place, :] = jnp.concatenate([wide_sum[:, :HD] + extra, wide_sum[:, HD:]], axis=1)

    def landing(n, step, j):
        s, g = n // KVL, n % KVL
        width = HEADS * HD
        return out.at[s, :, pl.ds(pl.multiple_of(j * QL + g * GROUP * HD + step * width, width), width)]

    def piece(n, step, j):
        width = HEADS * HD
        return mine.at[
            n, pl.ds(pl.multiple_of(j * ROWS, ROWS), ROWS), pl.ds(pl.multiple_of(step * width, width), width)
        ]

    def to_keeper(n, step, o):
        j, device = ring(o)
        return remote(
            piece(n, step, j), landing(n, step, kv), o_send.at[n, o, step], o_recv.at[n, kv, step], device
        )

    def to_self(n, step):
        return pltpu.make_async_copy(piece(n, step, kv), landing(n, step, kv), o_own.at[n, step])

    def from_ring(n, step, o):
        j = lax.rem(kv - o + 4, 4)
        landed = landing(n, step, j)
        return remote(landed, landed, o_send.at[n, o, step], o_recv.at[n, j, step], ring(o)[1])

    def finish(n):
        s, g = n // KVL, n % KVL
        for o in range(1, PLANE):
            from_plane(n, o, far, d_send, d_recv).wait_recv()
        total = jnp.concatenate([far[n, j] for j in range(PLANE)], axis=0)
        norm = jnp.broadcast_to(norms[n:n + 1, :], (HD, FEAT))
        hi, lo = split(jnp.concatenate([total, norm], axis=0))
        f_hi[...] = hi
        f_lo[...] = lo
        row = lax.broadcasted_iota(jnp.int32, (BLOCK, HD), 0)
        live = (row + anchor) >= starts_ref[s]

        @pl.loop(0, STEPS)
        def _(step):
            place = pl.ds(pl.multiple_of(step * HEADS * BLOCK, HEADS * BLOCK), HEADS * BLOCK)
            hi = p_hi[n, place, :]
            distant = mm(hi, f_hi[...], NT) + mm(p_lo[n, place, :], f_hi[...], NT) + mm(hi, f_lo[...], NT)
            close = near[n, place, :]
            for k in range(HEADS):
                head = step * HEADS + k
                a = jax.nn.sigmoid(jnp.full((1, HD), mix_ref[g * GROUP + head], F32))
                part = slice(k * BLOCK, (k + 1) * BLOCK)
                top_part = a * close[part, :HD] + (1.0 - a) * distant[part, :HD]
                bottom = a * close[part, HD:] + (1.0 - a) * distant[part, HD:]
                result = jnp.where(live, top_part / jnp.where(live, bottom, 1.0), 0.0)
                mine[n, :, pl.ds(pl.multiple_of(head * HD, HD), HD)] = result
            for o in (2, 1, 3):
                to_keeper(n, step, o).start()
            to_self(n, step).start()

    for n in range(COMBOS):
        for t in range(2):
            loads_own[n, t].wait()
        shift(n).start()
    window_own(0)
    load_km.wait()
    n_tx[...] = jnp.zeros((8, FEAT), F32)
    query_features(0)
    state(0)
    window_prev(0)
    window_own(1)
    state(1)
    window_prev(1)
    window_forward(0)
    window_own(2)
    state(2)
    window_prev(2)
    window_forward(1)
    window_relay(0)
    window_own(3)
    state(3)
    norm_start()
    window_prev(3)
    window_forward(2)
    window_relay(1)
    owner_total(0)
    window_forward(3)
    window_relay(2)
    query_features(1)
    owner_total(1)
    window_relay(3)
    query_features(2)
    owner_total(2)
    norm_total()
    query_features(3)
    owner_total(3)
    owner_prefix(0)
    attend_near(0)
    owner_prefix(1)
    norm_finish()
    finish(0)
    attend_near(1)
    owner_prefix(2)
    finish(1)
    attend_near(2)
    owner_prefix(3)
    finish(2)
    attend_near(3)
    finish(3)

    for n in range(COMBOS):
        shift(n).wait_send()
        to_partner(n, own).wait_send()
        for o in (1, 3):
            to_line(n, o, own).wait_send()
            forward(n, o).wait_send()
        relay_same(n).wait_send()
        relay_other(n).wait_send()
        for o in range(1, PLANE):
            to_owner(n, o).wait_send()
            to_reader(n, o).wait_send()
        for o in range(1, PLANES):
            @pl.when(z + o < PLANES)
            def _():
                to_later(n, o).wait_send()
    for o in range(1, PLANE):
        norm_to_plane(o).wait_send()
    for o in range(1, PLANES):
        @pl.when(z + o < PLANES)
        def _():
            norm_to_later(o).wait_send()
    for n in range(COMBOS):
        @pl.loop(0, STEPS)
        def _(step):
            to_self(n, step).wait()
            for o in range(1, 4):
                to_keeper(n, step, o).wait_send()
                from_ring(n, step, o).wait_recv()


def on_device(queries, keys, values, query_maps, key_maps, mix, window_blocks, starts):
    smem = pl.BlockSpec(memory_space=pltpu.SMEM)
    hbm = pl.BlockSpec(memory_space=pltpu.HBM)
    dma = pltpu.SemaphoreType.DMA
    vmem = pltpu.VMEM
    pieces = (COMBOS, PLANE, PIECE, FEAT)
    return pl.pallas_call(
        kernel,
        out_shape=jax.ShapeDtypeStruct((SEQS, ROWS, 4 * QL), F32),
        in_specs=[smem, smem, smem] + [hbm] * 5,
        out_specs=pl.BlockSpec(memory_space=pl.ANY),
        scratch_shapes=[
            vmem((COMBOS, BLOCK, GROUP * HD), F32),
            vmem((KVL * GROUP, HD, HALF), F32),
            vmem((KVL, HD, HALF), F32),
            vmem((COMBOS, 2, BLOCK, HD), F32),
            vmem((COMBOS, 2, BLOCK, HD), F32),
            vmem((COMBOS, PLANE, 2, BLOCK, HD), F32),
            vmem(pieces, F32),
            vmem(pieces, F32),
            vmem((COMBOS, PIECE, FEAT), F32),
            vmem(pieces, F32),
            vmem(pieces, F32),
            vmem(pieces, F32),
            vmem((COMBOS, GROUP * BLOCK, FEAT), BF16),
            vmem((COMBOS, GROUP * BLOCK, FEAT), BF16),
            vmem((COMBOS, GROUP * BLOCK, 2 * HD), F32),
            vmem((COMBOS, BLOCK, GROUP * HD), F32),
            vmem((WIN, 2 * HD), BF16),
            vmem((WIN, 2 * HD), BF16),
            vmem((WIN, 2 * HD), BF16),
            vmem((WIN, HD), BF16),
            vmem((2 * HD, FEAT), BF16),
            vmem((2 * HD, FEAT), BF16),
            vmem((8, FEAT), F32),
            vmem((PLANE, 8, FEAT), F32),
            vmem((8, FEAT), F32),
            vmem((PLANES, 8, FEAT), F32),
            vmem((8, FEAT), F32),
            dma((COMBOS, 2)), dma((COMBOS,)), dma((KVL,)), dma((1,)), dma((COMBOS,)), dma((COMBOS,)),
            dma((COMBOS, 7)), dma((COMBOS, 8)),
            dma((COMBOS, 8)), dma((COMBOS, 8)), dma((COMBOS, 8)), dma((COMBOS, 8)), dma((COMBOS, 8)), dma((COMBOS, 8)),
            dma((COMBOS, 4, STEPS)), dma((COMBOS, 4, STEPS)), dma((COMBOS, STEPS)),
            dma((8,)), dma((8,)), dma((8,)), dma((8,)),
        ],
        name="hybrid",
        compiler_params=pltpu.CompilerParams(
            collective_id=0, has_side_effects=True, vmem_limit_bytes=61 << 20
        ),
    )(starts, window_blocks.T, mix, queries, keys, values, query_maps, key_maps)


def solution(mesh):
    torus = Mesh(mesh.devices.reshape(8, 2, 4, 2, 2), ("ctx_0", "ctx_1", "ctx_2", "kv_0", "kv_1"))
    in_specs = (
        P(None, CTX, KV),
        P(None, CTX, KV),
        P(None, CTX, KV),
        P(KV, None, None),
        P(KV, None, None),
        P(KV),
        P(None, CTX),
        P(),
    )
    out_specs = P(None, CTX_KV, None)
    return jax.shard_map(
        on_device, mesh=torus, in_specs=in_specs, out_specs=out_specs, check_vma=False
    )
```

```python
import functools

import jax
import jax.numpy as jnp
from jax import lax
from jax.experimental import pallas as pl
from jax.experimental.pallas import tpu as pltpu
from jax.sharding import Mesh
from jax.sharding import PartitionSpec as P

HD = 128
HALF = 128
FEAT = 2 * HALF
BLOCK = 64
WBLK = 8
GROUP = 16
PLANE = 8
PLANES = 8
SEQS = 2
KVL = 2
COMBOS = SEQS * KVL
QL = KVL * GROUP * HD
WIN = 640
PIECE = 16
HEADS = 8
STEPS = GROUP // HEADS
ROWS = BLOCK // 4
NEG = -1e30
CTX = ("ctx_0", "ctx_1", "ctx_2")
KV = ("kv_0", "kv_1")
CTX_KV = CTX + KV
MESH = pl.DeviceIdType.MESH
F32 = jnp.float32
BF16 = jnp.bfloat16
HIGHEST = lax.Precision.HIGHEST

NN = (((1,), (0,)), ((), ()))
NT = (((1,), (1,)), ((), ()))
TN = (((0,), (0,)), ((), ()))


def remote(src, dst, send, recv, device):
    return pltpu.make_async_remote_copy(
        src_ref=src, dst_ref=dst, send_sem=send, recv_sem=recv, device_id=device, device_id_type=MESH
    )


def mm(a, b, dims):
    return lax.dot_general(a, b, dims, preferred_element_type=F32)


def split(x):
    hi = x.astype(BF16)
    return hi, (x - hi.astype(F32)).astype(BF16)


def softmax_pair(logits):
    up = jnp.exp(logits)
    down = jnp.exp(-logits)
    up = up / jnp.sum(up, axis=-1, keepdims=True)
    down = down / jnp.sum(down, axis=-1, keepdims=True)
    return jnp.concatenate([up, down], axis=-1)


def here():
    return [lax.axis_index(a) for a in CTX_KV]


def features(x, weights):
    x_hi, x_lo = split(x)
    w_hi, w_lo = split(weights)
    w = jnp.concatenate([w_hi, w_lo], axis=1)
    both = mm(jnp.concatenate([x_hi, x_lo], axis=1), jnp.concatenate([w, w], axis=0), NN)
    return both[:, :HALF] + both[:, HALF:]


def kernel(
    starts_ref, bits_ref, mix_ref, q_hbm, k_hbm, v_hbm, qm_hbm, km_hbm, out,
    q, qm, km, own, prev, kvw, a_tx, a_rx, t_tx, t_rx, d_tx, far, p_hi, p_lo, near, mine,
    k_hi, k_lo, v_both, f_both, n_tx, n_rx, m_tx, m_rx, norms,
    ld_own, ld_q, ld_qm, ld_km, z_send, z_recv, w_send, w_recv,
    a_send, a_recv, t_send, t_recv, d_send, d_recv, o_send, o_recv, o_own,
    n_send, n_recv, m_send, m_recv,
):
    z, x, y, h, c = here()
    me = x * 4 + y
    kv = h * 2 + c
    anchor = (z * PLANE + me) * BLOCK

    def lanes(n):
        return slice((n % KVL) * HD, (n % KVL + 1) * HD)

    def plane(o):
        j = lax.rem(me + o, PLANE)
        return j, (z, j // 4, lax.rem(j, 4), h, c)

    def column(o):
        j = lax.rem(z + o, PLANES)
        return j, (j, x, y, h, c)

    def line(o):
        j = lax.rem(y + o, 4)
        return j, (z, x, j, h, c)

    def ring(o):
        j = lax.rem(kv + o, 4)
        return j, (z, x, y, j // 2, lax.rem(j, 2))

    partner = (z, 1 - x, y, h, c)

    loads_own = {}
    for n in range(COMBOS):
        for t, hbm in enumerate((k_hbm, v_hbm)):
            loads_own[n, t] = pltpu.make_async_copy(hbm.at[n // KVL, :, lanes(n)], own.at[n, t], ld_own.at[n, t])
            loads_own[n, t].start()
    load_km = pltpu.make_async_copy(km_hbm, km, ld_km.at[0])
    load_km.start()
    loads_qm = []
    loads_q = []
    for g in range(KVL):
        loads_qm.append(
            pltpu.make_async_copy(qm_hbm.at[g * GROUP:(g + 1) * GROUP], qm.at[g * GROUP:(g + 1) * GROUP], ld_qm.at[g])
        )
    for n in range(COMBOS):
        g = n % KVL
        loads_q.append(
            pltpu.make_async_copy(q_hbm.at[n // KVL, :, g * GROUP * HD:(g + 1) * GROUP * HD], q.at[n], ld_q.at[n])
        )
    for copy in (loads_q[0], loads_q[2], loads_qm[0], loads_q[1], loads_q[3], loads_qm[1]):
        copy.start()

    barrier = pltpu.get_barrier_semaphore()
    greeted = [plane(o)[1] for o in range(1, PLANE)] + [column(o)[1] for o in range(1, PLANES)]
    greeted += [ring(o)[1] for o in range(1, 4)]
    for device in greeted:
        pl.semaphore_signal(barrier, inc=1, device_id=device, device_id_type=MESH)
    pl.semaphore_wait(barrier, len(greeted))

    def shift(n):
        return remote(own.at[n], prev.at[n], z_send.at[n], z_recv.at[n], column(1)[1])

    def to_line(n, o, source):
        return remote(source.at[n], kvw.at[n, me], w_send.at[n, o], w_recv.at[n, me], line(o)[1])

    def to_partner(n, source):
        return remote(source.at[n], kvw.at[n, me], w_send.at[n, 0], w_recv.at[n, me], partner)

    other = (1 - x) * 4 + y

    def forward(n, o):
        return remote(kvw.at[n, other], kvw.at[n, other], w_send.at[n, 3 + o], w_recv.at[n, other], line(o)[1])

    def window_own(n):
        @pl.when(x == 0)
        def _():
            to_partner(n, own).start()

        for o in (1, 3):
            @pl.when(y + o < 4)
            def _():
                to_line(n, o, own).start()

    def window_prev(n):
        @pl.when(x == 1)
        def _():
            to_partner(n, prev).start()

        for o in (1, 3):
            @pl.when(y + o >= 4)
            def _():
                to_line(n, o, prev).start()

        kvw[n, me] = prev[n]

    def arrived(n, slot):
        return remote(kvw.at[n, slot], kvw.at[n, slot], w_send.at[n, 0], w_recv.at[n, slot], partner)

    def window_forward(n):
        arrived(n, other).wait_recv()
        for o in (1, 3):
            forward(n, o).start()

    swing = 1 - 2 * lax.rem(y, 2)
    ahead = lax.rem(y + swing + 4, 4)
    behind = lax.rem(y - swing + 4, 4)

    def relay(n, slot, k, to):
        return remote(kvw.at[n, slot], kvw.at[n, slot], w_send.at[n, k], w_recv.at[n, slot], (z, x, to, h, c))

    def relay_same(n):
        return relay(n, x * 4 + behind, 2, ahead)

    def relay_other(n):
        return relay(n, (1 - x) * 4 + ahead, 5, behind)

    def window_relay(n):
        arrived(n, x * 4 + behind).wait_recv()
        relay_same(n).start()
        arrived(n, (1 - x) * 4 + ahead).wait_recv()
        relay_other(n).start()

    def to_owner(n, o):
        j, device = plane(o)
        return remote(a_tx.at[n, j], a_rx.at[n, me], a_send.at[n, o], a_recv.at[n, me], device)

    def state(n):
        s, g = n // KVL, n % KVL
        shift(n).wait_recv()
        phi = softmax_pair(features(prev[n, 0], km[g]))
        row = lax.broadcasted_iota(jnp.int32, (BLOCK, FEAT), 0)
        position = row + (anchor - PLANE * BLOCK)
        phi = jnp.where((position >= 0) & (position >= starts_ref[s]), phi, 0.0)
        hi, lo = split(phi)
        v_h, v_l = split(prev[n, 1])
        total = mm(jnp.concatenate([v_h, v_l], axis=0), jnp.concatenate([hi, hi], axis=0), TN) + mm(v_h, lo, TN)
        for j in range(PLANE):
            a_tx[n, j] = total[j * PIECE:(j + 1) * PIECE]
        n_tx[n:n + 1, :] = jnp.sum(phi, axis=0, keepdims=True)
        for o in range(1, PLANE):
            to_owner(n, o).start()
        a_rx[n, me] = a_tx[n, me]

    def norm_to_plane(o):
        return remote(n_tx, n_rx.at[me], n_send.at[o], n_recv.at[me], plane(o)[1])

    def norm_to_later(o):
        return remote(m_tx, m_rx.at[z], m_send.at[o], m_recv.at[z], column(o)[1])

    def norm_start():
        for o in range(1, PLANE):
            norm_to_plane(o).start()
        n_rx[me] = n_tx[...]

    def norm_total():
        for o in range(1, PLANE):
            j = lax.rem(me - o + PLANE, PLANE)
            remote(n_rx.at[j], n_rx.at[j], n_send.at[o], n_recv.at[j], plane(o)[1]).wait_recv()
        total = jnp.zeros((8, FEAT), F32)
        inside = jnp.zeros((8, FEAT), F32)
        for j in range(PLANE):
            total = total + n_rx[j]
            inside = jnp.where(j < me, total, inside)
        m_tx[...] = total
        norms[...] = inside
        for o in range(1, PLANES):
            @pl.when(z + o < PLANES)
            def _():
                norm_to_later(o).start()

    def norm_finish():
        for j in range(PLANES - 1):
            @pl.when(j < z)
            def _():
                remote(m_tx, m_rx.at[j], m_send.at[1], m_recv.at[j], partner).wait_recv()
                norms[...] = norms[...] + m_rx[j]

    def from_plane(n, o, buf, send, recv):
        j = lax.rem(me - o + PLANE, PLANE)
        return remote(buf.at[n, j], buf.at[n, j], send.at[n, o], recv.at[n, j], plane(o)[1])

    def to_later(n, o):
        return remote(t_tx.at[n], t_rx.at[n, z], t_send.at[n, o], t_recv.at[n, z], column(o)[1])

    def owner_total(n):
        for o in range(1, PLANE):
            from_plane(n, o, a_rx, a_send, a_recv).wait_recv()
        total = a_rx[n, 0]
        for j in range(1, PLANE):
            total = total + a_rx[n, j]
        t_tx[n] = total
        for o in range(1, PLANES):
            @pl.when(z + o < PLANES)
            def _():
                to_later(n, o).start()

    def to_reader(n, o):
        j, device = plane(o)
        return remote(d_tx.at[n, j], far.at[n, me], d_send.at[n, o], d_recv.at[n, me], device)

    def owner_prefix(n):
        d_tx[n, 0] = jnp.zeros((PIECE, FEAT), F32)
        for j in range(PLANES - 1):
            @pl.when(j < z)
            def _():
                remote(t_tx.at[n], t_rx.at[n, j], t_send.at[n, 1], t_recv.at[n, j], partner).wait_recv()
                d_tx[n, 0] = d_tx[n, 0] + t_rx[n, j]
        running = d_tx[n, 0]
        for j in range(PLANE - 1):
            running = running + a_rx[n, j]
            d_tx[n, j + 1] = running
        for o in range(1, PLANE):
            to_reader(n, o).start()
        far[n, me] = d_tx[n, me]

    def query_features(g):
        for n in (g, g + KVL):
            loads_q[n].wait()
        loads_qm[g].wait()

        @pl.loop(0, GROUP // 4)
        def _(step):
            span = pl.ds(pl.multiple_of(step * 4 * HD, 4 * HD), 4 * HD)
            wide = jnp.concatenate([q[g, :, span], q[g + KVL, :, span]], axis=0)
            logits = []
            for k in range(4):
                logits.append(features(wide[:, k * HD:(k + 1) * HD], qm[g * GROUP + step * 4 + k]))
            hi, lo = split(softmax_pair(jnp.concatenate(logits, axis=0)))
            for t in range(SEQS):
                for k in range(4):
                    place = pl.ds(pl.multiple_of((step * 4 + k) * BLOCK, BLOCK), BLOCK)
                    part = slice((k * SEQS + t) * BLOCK, (k * SEQS + t + 1) * BLOCK)
                    p_hi[t * KVL + g, place, :] = hi[part]
                    p_lo[t * KVL + g, place, :] = lo[part]

    def attend_near(n):
        s = n // KVL
        opposite = line(2)[0]
        for slot in (x * 4 + ahead, x * 4 + opposite, (1 - x) * 4 + behind, (1 - x) * 4 + opposite):
            arrived(n, slot).wait_recv()
        zeros = jnp.zeros((WIN - (WBLK + 1) * BLOCK, HD), F32)
        hi, lo = split(jnp.concatenate([kvw[n, j, 0] for j in range(PLANE)] + [own[n, 0], zeros], axis=0))
        k_hi[...] = jnp.concatenate([hi, hi], axis=1)
        k_lo[...] = jnp.concatenate([lo, lo], axis=1)
        hi, lo = split(jnp.concatenate([kvw[n, j, 1] for j in range(PLANE)] + [own[n, 1], zeros], axis=0))
        v_both[...] = jnp.concatenate([hi, lo], axis=1)
        start = starts_ref[s]
        column_id = lax.broadcasted_iota(jnp.int32, (8, WIN), 1)
        slot = column_id // BLOCK
        distance = jnp.where(slot < me, me - slot, me - slot + PLANE)
        bits = jnp.broadcast_to(bits_ref[0, s], (8, WIN))
        picked = lax.shift_right_logical(bits, jnp.maximum(distance - 1, 0)) & 1
        position = anchor - distance * BLOCK + (column_id & (BLOCK - 1))
        earlier = (slot < PLANE) & (picked == 1) & (position >= 0) & (position >= start)
        bias = jnp.where(earlier, 0.0, NEG)[:1, :WBLK * BLOCK]
        row = lax.broadcasted_iota(jnp.int32, (HEADS * BLOCK, HD), 0) & (BLOCK - 1)
        col = lax.broadcasted_iota(jnp.int32, (HEADS * BLOCK, HD), 1)
        own_bias = jnp.where((col <= row) & (anchor + col >= start), 0.0, NEG)

        @pl.loop(0, STEPS)
        def _(step):
            wide = q[n, :, pl.ds(pl.multiple_of(step * HEADS * HD, HEADS * HD), HEADS * HD)]
            rows = jnp.concatenate([wide[:, k * HD:(k + 1) * HD] for k in range(HEADS)], axis=0)
            q_hi, q_lo = split(rows * HD ** -0.5)
            both = jnp.concatenate([q_hi, q_lo], axis=1)
            scores = mm(both, k_hi[...], NT) + mm(both, k_lo[...], NT)
            scores = jnp.concatenate(
                [scores[:, :WBLK * BLOCK] + bias, scores[:, WBLK * BLOCK:] + own_bias], axis=1
            )
            top = jnp.max(scores, axis=1, keepdims=True)
            weights = jnp.exp(scores - top)
            e_hi, e_lo = split(weights)
            both = mm(e_hi, v_both[...], NN)
            close = both[:, :HD] + both[:, HD:] + mm(e_lo, v_both[:, :HD], NN)
            mass = jnp.broadcast_to(jnp.sum(weights, axis=1, keepdims=True), close.shape)
            place = pl.ds(pl.multiple_of(step * HEADS * BLOCK, HEADS * BLOCK), HEADS * BLOCK)
            near[n, place, :] = jnp.concatenate([close, mass], axis=1)

    def landing(n, step, j):
        s, g = n // KVL, n % KVL
        width = HEADS * HD
        return out.at[s, :, pl.ds(pl.multiple_of(j * QL + g * GROUP * HD + step * width, width), width)]

    def piece(n, step, j):
        width = HEADS * HD
        return mine.at[
            n, pl.ds(pl.multiple_of(j * ROWS, ROWS), ROWS), pl.ds(pl.multiple_of(step * width, width), width)
        ]

    def to_keeper(n, step, o):
        j, device = ring(o)
        return remote(
            piece(n, step, j), landing(n, step, kv), o_send.at[n, o, step], o_recv.at[n, kv, step], device
        )

    def to_self(n, step):
        return pltpu.make_async_copy(piece(n, step, kv), landing(n, step, kv), o_own.at[n, step])

    def from_ring(n, step, o):
        j = lax.rem(kv - o + 4, 4)
        landed = landing(n, step, j)
        return remote(landed, landed, o_send.at[n, o, step], o_recv.at[n, j, step], ring(o)[1])

    def finish(n):
        s, g = n // KVL, n % KVL
        for o in range(1, PLANE):
            from_plane(n, o, far, d_send, d_recv).wait_recv()
        total = jnp.concatenate([far[n, j] for j in range(PLANE)], axis=0)
        hi, lo = split(total)
        f_both[...] = jnp.concatenate([hi, lo], axis=0)
        norm = norms[n:n + 1, :]
        row = lax.broadcasted_iota(jnp.int32, (BLOCK, HD), 0)
        live = (row + anchor) >= starts_ref[s]

        @pl.loop(0, STEPS)
        def _(step):
            place = pl.ds(pl.multiple_of(step * HEADS * BLOCK, HEADS * BLOCK), HEADS * BLOCK)
            hi = p_hi[n, place, :]
            lo = p_lo[n, place, :]
            both = mm(hi, f_both[...], NT)
            distant = both[:, :HD] + both[:, HD:] + mm(lo, f_both[:HD, :], NT)
            seen = (hi.astype(F32) + lo.astype(F32)) * norm
            seen = jnp.sum(seen[:, :HALF] + seen[:, HALF:], axis=1, keepdims=True)
            seen = jnp.broadcast_to(seen, distant.shape)
            close = near[n, place, :]
            for k in range(HEADS):
                head = step * HEADS + k
                a = jax.nn.sigmoid(jnp.full((1, HD), mix_ref[g * GROUP + head], F32))
                part = slice(k * BLOCK, (k + 1) * BLOCK)
                top_part = a * close[part, :HD] + (1.0 - a) * distant[part, :HD]
                bottom = a * close[part, HD:] + (1.0 - a) * seen[part]
                result = jnp.where(live, top_part / jnp.where(live, bottom, 1.0), 0.0)
                mine[n, :, pl.ds(pl.multiple_of(head * HD, HD), HD)] = result
            for o in (2, 1, 3):
                to_keeper(n, step, o).start()
            to_self(n, step).start()

    for n in range(COMBOS):
        for t in range(2):
            loads_own[n, t].wait()
        shift(n).start()
    load_km.wait()
    n_tx[...] = jnp.zeros((8, FEAT), F32)
    window_own(0)
    query_features(0)
    state(0)
    window_prev(0)
    window_own(1)
    state(1)
    state(2)
    window_forward(0)
    state(3)
    norm_start()
    owner_total(0)
    window_prev(1)
    window_relay(0)
    owner_total(1)
    window_own(2)
    owner_total(2)
    window_forward(1)
    owner_total(3)
    window_prev(2)
    norm_total()
    query_features(1)
    window_relay(1)
    owner_prefix(0)
    window_forward(2)
    window_own(3)
    window_prev(3)
    attend_near(0)
    owner_prefix(1)
    norm_finish()
    finish(0)
    window_relay(2)
    owner_prefix(2)
    attend_near(1)
    finish(1)
    window_forward(3)
    owner_prefix(3)
    window_relay(3)
    attend_near(2)
    finish(2)
    attend_near(3)
    finish(3)

    for n in range(COMBOS):
        shift(n).wait_send()
        to_partner(n, own).wait_send()
        for o in (1, 3):
            to_line(n, o, own).wait_send()
            forward(n, o).wait_send()
        relay_same(n).wait_send()
        relay_other(n).wait_send()
        for o in range(1, PLANE):
            to_owner(n, o).wait_send()
            to_reader(n, o).wait_send()
        for o in range(1, PLANES):
            @pl.when(z + o < PLANES)
            def _():
                to_later(n, o).wait_send()
    for o in range(1, PLANE):
        norm_to_plane(o).wait_send()
    for o in range(1, PLANES):
        @pl.when(z + o < PLANES)
        def _():
            norm_to_later(o).wait_send()
    for n in range(COMBOS):
        @pl.loop(0, STEPS)
        def _(step):
            to_self(n, step).wait()
            for o in range(1, 4):
                to_keeper(n, step, o).wait_send()
                from_ring(n, step, o).wait_recv()


def on_device(queries, keys, values, query_maps, key_maps, mix, window_blocks, starts):
    smem = pl.BlockSpec(memory_space=pltpu.SMEM)
    hbm = pl.BlockSpec(memory_space=pltpu.HBM)
    dma = pltpu.SemaphoreType.DMA
    vmem = pltpu.VMEM
    pieces = (COMBOS, PLANE, PIECE, FEAT)
    return pl.pallas_call(
        kernel,
        out_shape=jax.ShapeDtypeStruct((SEQS, ROWS, 4 * QL), F32),
        in_specs=[smem, smem, smem] + [hbm] * 5,
        out_specs=pl.BlockSpec(memory_space=pl.ANY),
        scratch_shapes=[
            vmem((COMBOS, BLOCK, GROUP * HD), F32),
            vmem((KVL * GROUP, HD, HALF), F32),
            vmem((KVL, HD, HALF), F32),
            vmem((COMBOS, 2, BLOCK, HD), F32),
            vmem((COMBOS, 2, BLOCK, HD), F32),
            vmem((COMBOS, PLANE, 2, BLOCK, HD), F32),
            vmem(pieces, F32),
            vmem(pieces, F32),
            vmem((COMBOS, PIECE, FEAT), F32),
            vmem(pieces, F32),
            vmem(pieces, F32),
            vmem(pieces, F32),
            vmem((COMBOS, GROUP * BLOCK, FEAT), BF16),
            vmem((COMBOS, GROUP * BLOCK, FEAT), BF16),
            vmem((COMBOS, GROUP * BLOCK, 2 * HD), F32),
            vmem((COMBOS, BLOCK, GROUP * HD), F32),
            vmem((WIN, 2 * HD), BF16),
            vmem((WIN, 2 * HD), BF16),
            vmem((WIN, 2 * HD), BF16),
            vmem((2 * HD, FEAT), BF16),
            vmem((8, FEAT), F32),
            vmem((PLANE, 8, FEAT), F32),
            vmem((8, FEAT), F32),
            vmem((PLANES, 8, FEAT), F32),
            vmem((8, FEAT), F32),
            dma((COMBOS, 2)), dma((COMBOS,)), dma((KVL,)), dma((1,)), dma((COMBOS,)), dma((COMBOS,)),
            dma((COMBOS, 7)), dma((COMBOS, 8)),
            dma((COMBOS, 8)), dma((COMBOS, 8)), dma((COMBOS, 8)), dma((COMBOS, 8)), dma((COMBOS, 8)), dma((COMBOS, 8)),
            dma((COMBOS, 4, STEPS)), dma((COMBOS, 4, STEPS)), dma((COMBOS, STEPS)),
            dma((8,)), dma((8,)), dma((8,)), dma((8,)),
        ],
        name="hybrid",
        compiler_params=pltpu.CompilerParams(
            collective_id=0, has_side_effects=True, vmem_limit_bytes=61 << 20
        ),
    )(starts, window_blocks.T, mix, queries, keys, values, query_maps, key_maps)


def solution(mesh):
    torus = Mesh(mesh.devices.reshape(8, 2, 4, 2, 2), ("ctx_0", "ctx_1", "ctx_2", "kv_0", "kv_1"))
    in_specs = (
        P(None, CTX, KV),
        P(None, CTX, KV),
        P(None, CTX, KV),
        P(KV, None, None),
        P(KV, None, None),
        P(KV),
        P(None, CTX),
        P(),
    )
    out_specs = P(None, CTX_KV, None)
    return jax.shard_map(
        on_device, mesh=torus, in_specs=in_specs, out_specs=out_specs, check_vma=False
    )
```

```python
import functools

import jax
import jax.numpy as jnp
from jax import lax
from jax.experimental import pallas as pl
from jax.experimental.pallas import tpu as pltpu
from jax.sharding import Mesh
from jax.sharding import PartitionSpec as P

HD = 128
HALF = 128
FEAT = 2 * HALF
BLOCK = 64
WBLK = 8
GROUP = 16
PLANE = 8
PLANES = 8
SEQS = 2
KVL = 2
COMBOS = SEQS * KVL
QL = KVL * GROUP * HD
WIN = 640
PIECE = 16
HEADS = 8
STEPS = GROUP // HEADS
ROWS = BLOCK // 4
NEG = -1e30
CTX = ("ctx_0", "ctx_1", "ctx_2")
KV = ("kv_0", "kv_1")
CTX_KV = CTX + KV
MESH = pl.DeviceIdType.MESH
F32 = jnp.float32
BF16 = jnp.bfloat16
HIGHEST = lax.Precision.HIGHEST

NN = (((1,), (0,)), ((), ()))
NT = (((1,), (1,)), ((), ()))
TN = (((0,), (0,)), ((), ()))


def remote(src, dst, send, recv, device):
    return pltpu.make_async_remote_copy(
        src_ref=src, dst_ref=dst, send_sem=send, recv_sem=recv, device_id=device, device_id_type=MESH
    )


def mm(a, b, dims):
    return lax.dot_general(a, b, dims, preferred_element_type=F32)


def split(x):
    hi = x.astype(BF16)
    return hi, (x - hi.astype(F32)).astype(BF16)


def softmax_pair(logits):
    up = jnp.exp(logits)
    down = jnp.exp(-logits)
    up = up / jnp.sum(up, axis=-1, keepdims=True)
    down = down / jnp.sum(down, axis=-1, keepdims=True)
    return jnp.concatenate([up, down], axis=-1)


def here():
    return [lax.axis_index(a) for a in CTX_KV]


def features(x, weights):
    x_hi, x_lo = split(x)
    w_hi, w_lo = split(weights)
    w = jnp.concatenate([w_hi, w_lo], axis=1)
    both = mm(jnp.concatenate([x_hi, x_lo], axis=1), jnp.concatenate([w, w], axis=0), NN)
    return both[:, :HALF] + both[:, HALF:]


def kernel(
    starts_ref, bits_ref, mix_ref, q_hbm, k_hbm, v_hbm, qm_hbm, km_hbm, out,
    q, qm, km, own, prev, kvw, a_tx, a_rx, t_tx, t_rx, d_tx, far, p_hi, p_lo, near, mine,
    k_hi, k_lo, v_both, f_both, n_tx, n_rx, m_tx, m_rx, norms,
    ld_own, ld_q, ld_qm, ld_km, z_send, z_recv, w_send, w_recv,
    a_send, a_recv, t_send, t_recv, d_send, d_recv, o_send, o_recv, o_own,
    n_send, n_recv, m_send, m_recv,
):
    z, x, y, h, c = here()
    me = x * 4 + y
    kv = h * 2 + c
    anchor = (z * PLANE + me) * BLOCK

    def lanes(n):
        return slice((n % KVL) * HD, (n % KVL + 1) * HD)

    def plane(o):
        j = lax.rem(me + o, PLANE)
        return j, (z, j // 4, lax.rem(j, 4), h, c)

    def column(o):
        j = lax.rem(z + o, PLANES)
        return j, (j, x, y, h, c)

    def line(o):
        j = lax.rem(y + o, 4)
        return j, (z, x, j, h, c)

    def ring(o):
        j = lax.rem(kv + o, 4)
        return j, (z, x, y, j // 2, lax.rem(j, 2))

    partner = (z, 1 - x, y, h, c)

    barrier = pltpu.get_barrier_semaphore()
    greeted = [plane(o)[1] for o in range(1, PLANE)] + [column(o)[1] for o in range(1, PLANES)]
    greeted += [ring(o)[1] for o in range(1, 4)]
    for device in greeted:
        pl.semaphore_signal(barrier, inc=1, device_id=device, device_id_type=MESH)

    loads_own = {}
    for n in range(COMBOS):
        for t, hbm in enumerate((k_hbm, v_hbm)):
            loads_own[n, t] = pltpu.make_async_copy(hbm.at[n // KVL, :, lanes(n)], own.at[n, t], ld_own.at[n, t])
            loads_own[n, t].start()
    load_km = pltpu.make_async_copy(km_hbm, km, ld_km.at[0])
    load_km.start()
    loads_qm = []
    loads_q = []
    for g in range(KVL):
        loads_qm.append(
            pltpu.make_async_copy(qm_hbm.at[g * GROUP:(g + 1) * GROUP], qm.at[g * GROUP:(g + 1) * GROUP], ld_qm.at[g])
        )
    for n in range(COMBOS):
        g = n % KVL
        loads_q.append(
            pltpu.make_async_copy(q_hbm.at[n // KVL, :, g * GROUP * HD:(g + 1) * GROUP * HD], q.at[n], ld_q.at[n])
        )
    for copy in (loads_q[0], loads_q[2], loads_qm[0], loads_q[1], loads_q[3], loads_qm[1]):
        copy.start()

    pl.semaphore_wait(barrier, len(greeted))

    def shift(n):
        return remote(own.at[n], prev.at[n], z_send.at[n], z_recv.at[n], column(1)[1])

    def to_line(n, o, source):
        return remote(source.at[n], kvw.at[n, me], w_send.at[n, o], w_recv.at[n, me], line(o)[1])

    def to_partner(n, source):
        return remote(source.at[n], kvw.at[n, me], w_send.at[n, 0], w_recv.at[n, me], partner)

    other = (1 - x) * 4 + y

    def forward(n, o):
        return remote(kvw.at[n, other], kvw.at[n, other], w_send.at[n, 3 + o], w_recv.at[n, other], line(o)[1])

    def window_own(n):
        @pl.when(x == 0)
        def _():
            to_partner(n, own).start()

        for o in (1, 3):
            @pl.when(y + o < 4)
            def _():
                to_line(n, o, own).start()

    def window_prev(n):
        @pl.when(x == 1)
        def _():
            to_partner(n, prev).start()

        for o in (1, 3):
            @pl.when(y + o >= 4)
            def _():
                to_line(n, o, prev).start()

        kvw[n, me] = prev[n]

    def arrived(n, slot):
        return remote(kvw.at[n, slot], kvw.at[n, slot], w_send.at[n, 0], w_recv.at[n, slot], partner)

    def window_forward(n):
        arrived(n, other).wait_recv()
        for o in (1, 3):
            forward(n, o).start()

    swing = 1 - 2 * lax.rem(y, 2)
    ahead = lax.rem(y + swing + 4, 4)
    behind = lax.rem(y - swing + 4, 4)

    def relay(n, slot, k, to):
        return remote(kvw.at[n, slot], kvw.at[n, slot], w_send.at[n, k], w_recv.at[n, slot], (z, x, to, h, c))

    def relay_same(n):
        return relay(n, x * 4 + behind, 2, ahead)

    def relay_other(n):
        return relay(n, (1 - x) * 4 + ahead, 5, behind)

    def window_relay_same(n):
        arrived(n, x * 4 + behind).wait_recv()
        relay_same(n).start()

    def window_relay_other(n):
        arrived(n, (1 - x) * 4 + ahead).wait_recv()
        relay_other(n).start()

    def to_owner(n, o):
        j, device = plane(o)
        return remote(a_tx.at[n, j], a_rx.at[n, me], a_send.at[n, o], a_recv.at[n, me], device)

    def state(n):
        s, g = n // KVL, n % KVL
        shift(n).wait_recv()
        phi = softmax_pair(features(prev[n, 0], km[g]))
        row = lax.broadcasted_iota(jnp.int32, (BLOCK, FEAT), 0)
        position = row + (anchor - PLANE * BLOCK)
        phi = jnp.where((position >= 0) & (position >= starts_ref[s]), phi, 0.0)
        hi, lo = split(phi)
        v_h, v_l = split(prev[n, 1])
        total = mm(jnp.concatenate([v_h, v_l], axis=0), jnp.concatenate([hi, hi], axis=0), TN) + mm(v_h, lo, TN)
        for j in range(PLANE):
            a_tx[n, j] = total[j * PIECE:(j + 1) * PIECE]
        n_tx[n:n + 1, :] = jnp.sum(phi, axis=0, keepdims=True)
        for o in range(1, PLANE):
            to_owner(n, o).start()
        a_rx[n, me] = a_tx[n, me]

    def norm_to_plane(o):
        return remote(n_tx, n_rx.at[me], n_send.at[o], n_recv.at[me], plane(o)[1])

    def norm_to_later(o):
        return remote(m_tx, m_rx.at[z], m_send.at[o], m_recv.at[z], column(o)[1])

    def norm_start():
        for o in range(1, PLANE):
            norm_to_plane(o).start()
        n_rx[me] = n_tx[...]

    def norm_total():
        for o in range(1, PLANE):
            j = lax.rem(me - o + PLANE, PLANE)
            remote(n_rx.at[j], n_rx.at[j], n_send.at[o], n_recv.at[j], plane(o)[1]).wait_recv()
        total = jnp.zeros((8, FEAT), F32)
        inside = jnp.zeros((8, FEAT), F32)
        for j in range(PLANE):
            total = total + n_rx[j]
            inside = jnp.where(j < me, total, inside)
        m_tx[...] = total
        norms[...] = inside
        for o in range(1, PLANES - 1):
            @pl.when((z > 0) & (z + o < PLANES))
            def _():
                norm_to_later(o).start()

    def norm_finish():
        for j in range(1, PLANES - 1):
            @pl.when(j < z)
            def _():
                remote(m_tx, m_rx.at[j], m_send.at[1], m_recv.at[j], partner).wait_recv()
                norms[...] = norms[...] + m_rx[j]

    def from_plane(n, o, buf, send, recv):
        j = lax.rem(me - o + PLANE, PLANE)
        return remote(buf.at[n, j], buf.at[n, j], send.at[n, o], recv.at[n, j], plane(o)[1])

    def to_later(n, o):
        return remote(t_tx.at[n], t_rx.at[n, z], t_send.at[n, o], t_recv.at[n, z], column(o)[1])

    def owner_total(n):
        for o in range(1, PLANE):
            from_plane(n, o, a_rx, a_send, a_recv).wait_recv()
        total = a_rx[n, 0]
        for j in range(1, PLANE):
            total = total + a_rx[n, j]
        t_tx[n] = total
        for o in range(1, PLANES - 1):
            @pl.when((z > 0) & (z + o < PLANES))
            def _():
                to_later(n, o).start()

    def to_reader(n, o):
        j, device = plane(o)
        return remote(d_tx.at[n, j], far.at[n, me], d_send.at[n, o], d_recv.at[n, me], device)

    def owner_prefix(n):
        d_tx[n, 0] = jnp.zeros((PIECE, FEAT), F32)
        for j in range(1, PLANES - 1):
            @pl.when(j < z)
            def _():
                remote(t_tx.at[n], t_rx.at[n, j], t_send.at[n, 1], t_recv.at[n, j], partner).wait_recv()
                d_tx[n, 0] = d_tx[n, 0] + t_rx[n, j]
        running = d_tx[n, 0]
        for j in range(PLANE - 1):
            running = running + a_rx[n, j]
            d_tx[n, j + 1] = running
        for o in range(1, PLANE):
            to_reader(n, o).start()
        far[n, me] = d_tx[n, me]

    def query_features(g):
        for n in (g, g + KVL):
            loads_q[n].wait()
        loads_qm[g].wait()

        @pl.loop(0, GROUP // 4)
        def _(step):
            span = pl.ds(pl.multiple_of(step * 4 * HD, 4 * HD), 4 * HD)
            wide = jnp.concatenate([q[g, :, span], q[g + KVL, :, span]], axis=0)
            logits = []
            for k in range(4):
                logits.append(features(wide[:, k * HD:(k + 1) * HD], qm[g * GROUP + step * 4 + k]))
            hi, lo = split(softmax_pair(jnp.concatenate(logits, axis=0)))
            for t in range(SEQS):
                for k in range(4):
                    place = pl.ds(pl.multiple_of((step * 4 + k) * BLOCK, BLOCK), BLOCK)
                    part = slice((k * SEQS + t) * BLOCK, (k * SEQS + t + 1) * BLOCK)
                    p_hi[t * KVL + g, place, :] = hi[part]
                    p_lo[t * KVL + g, place, :] = lo[part]

    def attend_near(n):
        s = n // KVL
        opposite = line(2)[0]
        for slot in (x * 4 + ahead, x * 4 + opposite, (1 - x) * 4 + behind, (1 - x) * 4 + opposite):
            arrived(n, slot).wait_recv()
        zeros = jnp.zeros((WIN - (WBLK + 1) * BLOCK, HD), F32)
        hi, lo = split(jnp.concatenate([kvw[n, j, 0] for j in range(PLANE)] + [own[n, 0], zeros], axis=0))
        k_hi[...] = jnp.concatenate([hi, hi], axis=1)
        k_lo[...] = jnp.concatenate([lo, lo], axis=1)
        hi, lo = split(jnp.concatenate([kvw[n, j, 1] for j in range(PLANE)] + [own[n, 1], zeros], axis=0))
        v_both[...] = jnp.concatenate([hi, lo], axis=1)
        start = starts_ref[s]
        column_id = lax.broadcasted_iota(jnp.int32, (8, WIN), 1)
        slot = column_id // BLOCK
        distance = jnp.where(slot < me, me - slot, me - slot + PLANE)
        bits = jnp.broadcast_to(bits_ref[0, s], (8, WIN))
        picked = lax.shift_right_logical(bits, jnp.maximum(distance - 1, 0)) & 1
        position = anchor - distance * BLOCK + (column_id & (BLOCK - 1))
        earlier = (slot < PLANE) & (picked == 1) & (position >= 0) & (position >= start)
        bias = jnp.where(earlier, 0.0, NEG)[:1, :WBLK * BLOCK]
        row = lax.broadcasted_iota(jnp.int32, (HEADS * BLOCK, HD), 0) & (BLOCK - 1)
        col = lax.broadcasted_iota(jnp.int32, (HEADS * BLOCK, HD), 1)
        own_bias = jnp.where((col <= row) & (anchor + col >= start), 0.0, NEG)

        @pl.loop(0, STEPS)
        def _(step):
            wide = q[n, :, pl.ds(pl.multiple_of(step * HEADS * HD, HEADS * HD), HEADS * HD)]
            rows = jnp.concatenate([wide[:, k * HD:(k + 1) * HD] for k in range(HEADS)], axis=0)
            q_hi, q_lo = split(rows * HD ** -0.5)
            both = jnp.concatenate([q_hi, q_lo], axis=1)
            scores = mm(both, k_hi[...], NT) + mm(both, k_lo[...], NT)
            scores = jnp.concatenate(
                [scores[:, :WBLK * BLOCK] + bias, scores[:, WBLK * BLOCK:] + own_bias], axis=1
            )
            top = jnp.max(scores, axis=1, keepdims=True)
            weights = jnp.exp(scores - top)
            e_hi, e_lo = split(weights)
            both = mm(e_hi, v_both[...], NN)
            close = both[:, :HD] + both[:, HD:] + mm(e_lo, v_both[:, :HD], NN)
            mass = jnp.broadcast_to(jnp.sum(weights, axis=1, keepdims=True), close.shape)
            place = pl.ds(pl.multiple_of(step * HEADS * BLOCK, HEADS * BLOCK), HEADS * BLOCK)
            near[n, place, :] = jnp.concatenate([close, mass], axis=1)

    def landing(n, step, j):
        s, g = n // KVL, n % KVL
        width = HEADS * HD
        return out.at[s, :, pl.ds(pl.multiple_of(j * QL + g * GROUP * HD + step * width, width), width)]

    def piece(n, step, j):
        width = HEADS * HD
        return mine.at[
            n, pl.ds(pl.multiple_of(j * ROWS, ROWS), ROWS), pl.ds(pl.multiple_of(step * width, width), width)
        ]

    def to_keeper(n, step, o):
        j, device = ring(o)
        return remote(
            piece(n, step, j), landing(n, step, kv), o_send.at[n, o, step], o_recv.at[n, kv, step], device
        )

    def to_self(n, step):
        return pltpu.make_async_copy(piece(n, step, kv), landing(n, step, kv), o_own.at[n, step])

    def from_ring(n, step, o):
        j = lax.rem(kv - o + 4, 4)
        landed = landing(n, step, j)
        return remote(landed, landed, o_send.at[n, o, step], o_recv.at[n, j, step], ring(o)[1])

    def finish(n):
        s, g = n // KVL, n % KVL
        for o in range(1, PLANE):
            from_plane(n, o, far, d_send, d_recv).wait_recv()
        total = jnp.concatenate([far[n, j] for j in range(PLANE)], axis=0)
        hi, lo = split(total)
        f_both[...] = jnp.concatenate([hi, lo], axis=0)
        norm = norms[n:n + 1, :]
        row = lax.broadcasted_iota(jnp.int32, (BLOCK, HD), 0)
        live = (row + anchor) >= starts_ref[s]

        @pl.loop(0, STEPS)
        def _(step):
            place = pl.ds(pl.multiple_of(step * HEADS * BLOCK, HEADS * BLOCK), HEADS * BLOCK)
            hi = p_hi[n, place, :]
            lo = p_lo[n, place, :]
            both = mm(hi, f_both[...], NT)
            distant = both[:, :HD] + both[:, HD:] + mm(lo, f_both[:HD, :], NT)
            seen = (hi.astype(F32) + lo.astype(F32)) * norm
            seen = jnp.sum(seen[:, :HALF] + seen[:, HALF:], axis=1, keepdims=True)
            seen = jnp.broadcast_to(seen, distant.shape)
            close = near[n, place, :]
            for k in range(HEADS):
                head = step * HEADS + k
                a = jax.nn.sigmoid(jnp.full((1, HD), mix_ref[g * GROUP + head], F32))
                part = slice(k * BLOCK, (k + 1) * BLOCK)
                top_part = a * close[part, :HD] + (1.0 - a) * distant[part, :HD]
                bottom = a * close[part, HD:] + (1.0 - a) * seen[part]
                result = jnp.where(live, top_part / jnp.where(live, bottom, 1.0), 0.0)
                mine[n, :, pl.ds(pl.multiple_of(head * HD, HD), HD)] = result
            for o in (2, 1, 3):
                to_keeper(n, step, o).start()
            to_self(n, step).start()

    for n in range(COMBOS):
        for t in range(2):
            loads_own[n, t].wait()
        shift(n).start()
    load_km.wait()
    n_tx[...] = jnp.zeros((8, FEAT), F32)
    window_own(0)
    query_features(0)
    state(0)
    window_prev(0)
    window_own(1)
    state(1)
    state(2)
    window_forward(0)
    state(3)
    norm_start()
    owner_total(0)
    window_prev(1)
    window_relay_same(0)
    window_relay_other(0)
    owner_total(1)
    window_own(2)
    owner_total(2)
    window_forward(1)
    owner_total(3)
    window_prev(2)
    norm_total()
    query_features(1)
    window_relay_same(1)
    window_relay_other(1)
    owner_prefix(0)
    window_forward(2)
    window_own(3)
    window_prev(3)
    owner_prefix(1)
    norm_finish()
    attend_near(0)
    owner_prefix(2)
    finish(0)
    window_relay_same(2)
    window_relay_other(2)
    window_forward(3)
    attend_near(1)
    owner_prefix(3)
    finish(1)
    window_relay_same(3)
    window_relay_other(3)
    attend_near(2)
    finish(2)
    attend_near(3)
    finish(3)

    for n in range(COMBOS):
        shift(n).wait_send()
        to_partner(n, own).wait_send()
        for o in (1, 3):
            to_line(n, o, own).wait_send()
            forward(n, o).wait_send()
        relay_same(n).wait_send()
        relay_other(n).wait_send()
        for o in range(1, PLANE):
            to_owner(n, o).wait_send()
            to_reader(n, o).wait_send()
        for o in range(1, PLANES - 1):
            @pl.when((z > 0) & (z + o < PLANES))
            def _():
                to_later(n, o).wait_send()
    for o in range(1, PLANE):
        norm_to_plane(o).wait_send()
    for o in range(1, PLANES - 1):
        @pl.when((z > 0) & (z + o < PLANES))
        def _():
            norm_to_later(o).wait_send()
    for n in range(COMBOS):
        @pl.loop(0, STEPS)
        def _(step):
            to_self(n, step).wait()
            for o in range(1, 4):
                to_keeper(n, step, o).wait_send()
                from_ring(n, step, o).wait_recv()


def on_device(queries, keys, values, query_maps, key_maps, mix, window_blocks, starts):
    smem = pl.BlockSpec(memory_space=pltpu.SMEM)
    hbm = pl.BlockSpec(memory_space=pltpu.HBM)
    dma = pltpu.SemaphoreType.DMA
    vmem = pltpu.VMEM
    pieces = (COMBOS, PLANE, PIECE, FEAT)
    return pl.pallas_call(
        kernel,
        out_shape=jax.ShapeDtypeStruct((SEQS, ROWS, 4 * QL), F32),
        in_specs=[smem, smem, smem] + [hbm] * 5,
        out_specs=pl.BlockSpec(memory_space=pl.ANY),
        scratch_shapes=[
            vmem((COMBOS, BLOCK, GROUP * HD), F32),
            vmem((KVL * GROUP, HD, HALF), F32),
            vmem((KVL, HD, HALF), F32),
            vmem((COMBOS, 2, BLOCK, HD), F32),
            vmem((COMBOS, 2, BLOCK, HD), F32),
            vmem((COMBOS, PLANE, 2, BLOCK, HD), F32),
            vmem(pieces, F32),
            vmem(pieces, F32),
            vmem((COMBOS, PIECE, FEAT), F32),
            vmem(pieces, F32),
            vmem(pieces, F32),
            vmem(pieces, F32),
            vmem((COMBOS, GROUP * BLOCK, FEAT), BF16),
            vmem((COMBOS, GROUP * BLOCK, FEAT), BF16),
            vmem((COMBOS, GROUP * BLOCK, 2 * HD), F32),
            vmem((COMBOS, BLOCK, GROUP * HD), F32),
            vmem((WIN, 2 * HD), BF16),
            vmem((WIN, 2 * HD), BF16),
            vmem((WIN, 2 * HD), BF16),
            vmem((2 * HD, FEAT), BF16),
            vmem((8, FEAT), F32),
            vmem((PLANE, 8, FEAT), F32),
            vmem((8, FEAT), F32),
            vmem((PLANES, 8, FEAT), F32),
            vmem((8, FEAT), F32),
            dma((COMBOS, 2)), dma((COMBOS,)), dma((KVL,)), dma((1,)), dma((COMBOS,)), dma((COMBOS,)),
            dma((COMBOS, 7)), dma((COMBOS, 8)),
            dma((COMBOS, 8)), dma((COMBOS, 8)), dma((COMBOS, 8)), dma((COMBOS, 8)), dma((COMBOS, 8)), dma((COMBOS, 8)),
            dma((COMBOS, 4, STEPS)), dma((COMBOS, 4, STEPS)), dma((COMBOS, STEPS)),
            dma((8,)), dma((8,)), dma((8,)), dma((8,)),
        ],
        name="hybrid",
        compiler_params=pltpu.CompilerParams(
            collective_id=0, has_side_effects=True, vmem_limit_bytes=61 << 20
        ),
    )(starts, window_blocks.T, mix, queries, keys, values, query_maps, key_maps)


def solution(mesh):
    torus = Mesh(mesh.devices.reshape(8, 2, 4, 2, 2), ("ctx_0", "ctx_1", "ctx_2", "kv_0", "kv_1"))
    in_specs = (
        P(None, CTX, KV),
        P(None, CTX, KV),
        P(None, CTX, KV),
        P(KV, None, None),
        P(KV, None, None),
        P(KV),
        P(None, CTX),
        P(),
    )
    out_specs = P(None, CTX_KV, None)
    return jax.shard_map(
        on_device, mesh=torus, in_specs=in_specs, out_specs=out_specs, check_vma=False
    )
```

```python
import functools

import jax
import jax.numpy as jnp
from jax import lax
from jax.experimental import pallas as pl
from jax.experimental.pallas import tpu as pltpu
from jax.sharding import Mesh
from jax.sharding import PartitionSpec as P

HD = 128
HALF = 128
FEAT = 2 * HALF
BLOCK = 64
WBLK = 8
GROUP = 16
PLANE = 8
PLANES = 8
SEQS = 2
KVL = 2
COMBOS = SEQS * KVL
QL = KVL * GROUP * HD
WIN = 640
PIECE = 16
HEADS = 16
STEPS = GROUP // HEADS
ROWS = BLOCK // 4
NEG = -1e30
CTX = ("ctx_0", "ctx_1", "ctx_2")
KV = ("kv_0", "kv_1")
CTX_KV = CTX + KV
MESH = pl.DeviceIdType.MESH
F32 = jnp.float32
BF16 = jnp.bfloat16
HIGHEST = lax.Precision.HIGHEST

NN = (((1,), (0,)), ((), ()))
NT = (((1,), (1,)), ((), ()))
TN = (((0,), (0,)), ((), ()))


def remote(src, dst, send, recv, device):
    return pltpu.make_async_remote_copy(
        src_ref=src, dst_ref=dst, send_sem=send, recv_sem=recv, device_id=device, device_id_type=MESH
    )


def mm(a, b, dims):
    return lax.dot_general(a, b, dims, preferred_element_type=F32)


def split(x):
    hi = x.astype(BF16)
    return hi, (x - hi.astype(F32)).astype(BF16)


def softmax_pair(logits):
    up = jnp.exp(logits)
    down = jnp.exp(-logits)
    up = up / jnp.sum(up, axis=-1, keepdims=True)
    down = down / jnp.sum(down, axis=-1, keepdims=True)
    return jnp.concatenate([up, down], axis=-1)


def here():
    return [lax.axis_index(a) for a in CTX_KV]


def features(x, weights):
    x_hi, x_lo = split(x)
    w_hi, w_lo = split(weights)
    w = jnp.concatenate([w_hi, w_lo], axis=1)
    both = mm(jnp.concatenate([x_hi, x_lo], axis=1), jnp.concatenate([w, w], axis=0), NN)
    return both[:, :HALF] + both[:, HALF:]


def kernel(
    starts_ref, bits_ref, mix_ref, q_hbm, k_hbm, v_hbm, qm_hbm, km_hbm, out,
    q, qm, km, own, prev, kvw, a_tx, a_rx, t_tx, t_rx, d_tx, far, p_hi, p_lo, near, mine,
    k_hi, k_lo, v_both, f_both, n_tx, n_rx, m_tx, m_rx, norms,
    ld_own, ld_q, ld_qm, ld_km, z_send, z_recv, w_send, w_recv,
    a_send, a_recv, t_send, t_recv, d_send, d_recv, o_send, o_recv, o_own,
    n_send, n_recv, m_send, m_recv,
):
    z, x, y, h, c = here()
    me = x * 4 + y
    kv = h * 2 + c
    anchor = (z * PLANE + me) * BLOCK

    def lanes(n):
        return slice((n % KVL) * HD, (n % KVL + 1) * HD)

    def plane(o):
        j = lax.rem(me + o, PLANE)
        return j, (z, j // 4, lax.rem(j, 4), h, c)

    def column(o):
        j = lax.rem(z + o, PLANES)
        return j, (j, x, y, h, c)

    def line(o):
        j = lax.rem(y + o, 4)
        return j, (z, x, j, h, c)

    def ring(o):
        j = lax.rem(kv + o, 4)
        return j, (z, x, y, j // 2, lax.rem(j, 2))

    partner = (z, 1 - x, y, h, c)

    barrier = pltpu.get_barrier_semaphore()
    greeted = [plane(o)[1] for o in range(1, PLANE)] + [column(o)[1] for o in range(1, PLANES)]
    greeted += [ring(o)[1] for o in range(1, 4)]
    for device in greeted:
        pl.semaphore_signal(barrier, inc=1, device_id=device, device_id_type=MESH)

    loads_own = {}
    for n in range(COMBOS):
        for t, hbm in enumerate((k_hbm, v_hbm)):
            loads_own[n, t] = pltpu.make_async_copy(hbm.at[n // KVL, :, lanes(n)], own.at[n, t], ld_own.at[n, t])
            loads_own[n, t].start()
    load_km = pltpu.make_async_copy(km_hbm, km, ld_km.at[0])
    load_km.start()
    loads_qm = []
    loads_q = []
    for g in range(KVL):
        loads_qm.append(
            pltpu.make_async_copy(qm_hbm.at[g * GROUP:(g + 1) * GROUP], qm.at[g * GROUP:(g + 1) * GROUP], ld_qm.at[g])
        )
    for n in range(COMBOS):
        g = n % KVL
        loads_q.append(
            pltpu.make_async_copy(q_hbm.at[n // KVL, :, g * GROUP * HD:(g + 1) * GROUP * HD], q.at[n], ld_q.at[n])
        )
    for copy in (loads_q[0], loads_q[2], loads_qm[0], loads_q[1], loads_q[3], loads_qm[1]):
        copy.start()

    pl.semaphore_wait(barrier, len(greeted))

    def shift(n):
        return remote(own.at[n], prev.at[n], z_send.at[n], z_recv.at[n], column(1)[1])

    def to_line(n, o, source):
        return remote(source.at[n], kvw.at[n, me], w_send.at[n, o], w_recv.at[n, me], line(o)[1])

    def to_partner(n, source):
        return remote(source.at[n], kvw.at[n, me], w_send.at[n, 0], w_recv.at[n, me], partner)

    other = (1 - x) * 4 + y

    def forward(n, o):
        return remote(kvw.at[n, other], kvw.at[n, other], w_send.at[n, 3 + o], w_recv.at[n, other], line(o)[1])

    def window_own(n):
        @pl.when(x == 0)
        def _():
            to_partner(n, own).start()

        for o in (1, 3):
            @pl.when(y + o < 4)
            def _():
                to_line(n, o, own).start()

    def window_prev(n):
        @pl.when(x == 1)
        def _():
            to_partner(n, prev).start()

        for o in (1, 3):
            @pl.when(y + o >= 4)
            def _():
                to_line(n, o, prev).start()

        kvw[n, me] = prev[n]

    def arrived(n, slot):
        return remote(kvw.at[n, slot], kvw.at[n, slot], w_send.at[n, 0], w_recv.at[n, slot], partner)

    def window_forward(n):
        arrived(n, other).wait_recv()
        for o in (1, 3):
            forward(n, o).start()

    swing = 1 - 2 * lax.rem(y, 2)
    ahead = lax.rem(y + swing + 4, 4)
    behind = lax.rem(y - swing + 4, 4)

    def relay(n, slot, k, to):
        return remote(kvw.at[n, slot], kvw.at[n, slot], w_send.at[n, k], w_recv.at[n, slot], (z, x, to, h, c))

    def relay_same(n):
        return relay(n, x * 4 + behind, 2, ahead)

    def relay_other(n):
        return relay(n, (1 - x) * 4 + ahead, 5, behind)

    def window_relay_same(n):
        arrived(n, x * 4 + behind).wait_recv()
        relay_same(n).start()

    def window_relay_other(n):
        arrived(n, (1 - x) * 4 + ahead).wait_recv()
        relay_other(n).start()

    def to_owner(n, o):
        j, device = plane(o)
        return remote(a_tx.at[n, j], a_rx.at[n, me], a_send.at[n, o], a_recv.at[n, me], device)

    def state(n):
        s, g = n // KVL, n % KVL
        shift(n).wait_recv()
        phi = softmax_pair(features(prev[n, 0], km[g]))
        row = lax.broadcasted_iota(jnp.int32, (BLOCK, FEAT), 0)
        position = row + (anchor - PLANE * BLOCK)
        phi = jnp.where((position >= 0) & (position >= starts_ref[s]), phi, 0.0)
        hi, lo = split(phi)
        v_h, v_l = split(prev[n, 1])
        total = mm(jnp.concatenate([v_h, v_l], axis=0), jnp.concatenate([hi, hi], axis=0), TN) + mm(v_h, lo, TN)
        for j in range(PLANE):
            a_tx[n, j] = total[j * PIECE:(j + 1) * PIECE]
        n_tx[n:n + 1, :] = jnp.sum(phi, axis=0, keepdims=True)
        for o in range(1, PLANE):
            to_owner(n, o).start()
        a_rx[n, me] = a_tx[n, me]

    def norm_to_plane(o):
        return remote(n_tx, n_rx.at[me], n_send.at[o], n_recv.at[me], plane(o)[1])

    def norm_to_later(o):
        return remote(m_tx, m_rx.at[z], m_send.at[o], m_recv.at[z], column(o)[1])

    def norm_start():
        for o in range(1, PLANE):
            norm_to_plane(o).start()
        n_rx[me] = n_tx[...]

    def norm_total():
        for o in range(1, PLANE):
            j = lax.rem(me - o + PLANE, PLANE)
            remote(n_rx.at[j], n_rx.at[j], n_send.at[o], n_recv.at[j], plane(o)[1]).wait_recv()
        total = jnp.zeros((8, FEAT), F32)
        inside = jnp.zeros((8, FEAT), F32)
        for j in range(PLANE):
            total = total + n_rx[j]
            inside = jnp.where(j < me, total, inside)
        m_tx[...] = total
        norms[...] = inside
        for o in range(1, PLANES - 1):
            @pl.when((z > 0) & (z + o < PLANES))
            def _():
                norm_to_later(o).start()

    def norm_finish():
        for j in range(1, PLANES - 1):
            @pl.when(j < z)
            def _():
                remote(m_tx, m_rx.at[j], m_send.at[1], m_recv.at[j], partner).wait_recv()
                norms[...] = norms[...] + m_rx[j]

    def from_plane(n, o, buf, send, recv):
        j = lax.rem(me - o + PLANE, PLANE)
        return remote(buf.at[n, j], buf.at[n, j], send.at[n, o], recv.at[n, j], plane(o)[1])

    def to_later(n, o):
        return remote(t_tx.at[n], t_rx.at[n, z], t_send.at[n, o], t_recv.at[n, z], column(o)[1])

    def owner_total(n):
        for o in range(1, PLANE):
            from_plane(n, o, a_rx, a_send, a_recv).wait_recv()
        total = a_rx[n, 0]
        for j in range(1, PLANE):
            total = total + a_rx[n, j]
        t_tx[n] = total
        for o in range(1, PLANES - 1):
            @pl.when((z > 0) & (z + o < PLANES))
            def _():
                to_later(n, o).start()

    def to_reader(n, o):
        j, device = plane(o)
        return remote(d_tx.at[n, j], far.at[n, me], d_send.at[n, o], d_recv.at[n, me], device)

    def owner_prefix(n):
        d_tx[n, 0] = jnp.zeros((PIECE, FEAT), F32)
        for j in range(1, PLANES - 1):
            @pl.when(j < z)
            def _():
                remote(t_tx.at[n], t_rx.at[n, j], t_send.at[n, 1], t_recv.at[n, j], partner).wait_recv()
                d_tx[n, 0] = d_tx[n, 0] + t_rx[n, j]
        running = d_tx[n, 0]
        for j in range(PLANE - 1):
            running = running + a_rx[n, j]
            d_tx[n, j + 1] = running
        for o in range(1, PLANE):
            to_reader(n, o).start()
        far[n, me] = d_tx[n, me]

    def query_features(g):
        for n in (g, g + KVL):
            loads_q[n].wait()
        loads_qm[g].wait()

        @pl.loop(0, GROUP // 4)
        def _(step):
            span = pl.ds(pl.multiple_of(step * 4 * HD, 4 * HD), 4 * HD)
            wide = jnp.concatenate([q[g, :, span], q[g + KVL, :, span]], axis=0)
            logits = []
            for k in range(4):
                logits.append(features(wide[:, k * HD:(k + 1) * HD], qm[g * GROUP + step * 4 + k]))
            hi, lo = split(softmax_pair(jnp.concatenate(logits, axis=0)))
            for t in range(SEQS):
                for k in range(4):
                    place = pl.ds(pl.multiple_of((step * 4 + k) * BLOCK, BLOCK), BLOCK)
                    part = slice((k * SEQS + t) * BLOCK, (k * SEQS + t + 1) * BLOCK)
                    p_hi[t * KVL + g, place, :] = hi[part]
                    p_lo[t * KVL + g, place, :] = lo[part]

    def attend_near(n):
        s = n // KVL
        opposite = line(2)[0]
        for slot in (x * 4 + ahead, x * 4 + opposite, (1 - x) * 4 + behind, (1 - x) * 4 + opposite):
            arrived(n, slot).wait_recv()
        zeros = jnp.zeros((WIN - (WBLK + 1) * BLOCK, HD), F32)
        hi, lo = split(jnp.concatenate([kvw[n, j, 0] for j in range(PLANE)] + [own[n, 0], zeros], axis=0))
        k_hi[...] = jnp.concatenate([hi, hi], axis=1)
        k_lo[...] = jnp.concatenate([lo, lo], axis=1)
        hi, lo = split(jnp.concatenate([kvw[n, j, 1] for j in range(PLANE)] + [own[n, 1], zeros], axis=0))
        v_both[...] = jnp.concatenate([hi, lo], axis=1)
        start = starts_ref[s]
        column_id = lax.broadcasted_iota(jnp.int32, (8, WIN), 1)
        slot = column_id // BLOCK
        distance = jnp.where(slot < me, me - slot, me - slot + PLANE)
        bits = jnp.broadcast_to(bits_ref[0, s], (8, WIN))
        picked = lax.shift_right_logical(bits, jnp.maximum(distance - 1, 0)) & 1
        position = anchor - distance * BLOCK + (column_id & (BLOCK - 1))
        earlier = (slot < PLANE) & (picked == 1) & (position >= 0) & (position >= start)
        bias = jnp.where(earlier, 0.0, NEG)[:1, :WBLK * BLOCK]
        row = lax.broadcasted_iota(jnp.int32, (HEADS * BLOCK, HD), 0) & (BLOCK - 1)
        col = lax.broadcasted_iota(jnp.int32, (HEADS * BLOCK, HD), 1)
        own_bias = jnp.where((col <= row) & (anchor + col >= start), 0.0, NEG)

        @pl.loop(0, STEPS)
        def _(step):
            wide = q[n, :, pl.ds(pl.multiple_of(step * HEADS * HD, HEADS * HD), HEADS * HD)]
            rows = jnp.concatenate([wide[:, k * HD:(k + 1) * HD] for k in range(HEADS)], axis=0)
            q_hi, q_lo = split(rows * HD ** -0.5)
            both = jnp.concatenate([q_hi, q_lo], axis=1)
            scores = mm(both, k_hi[...], NT) + mm(both, k_lo[...], NT)
            scores = jnp.concatenate(
                [scores[:, :WBLK * BLOCK] + bias, scores[:, WBLK * BLOCK:] + own_bias], axis=1
            )
            top = jnp.max(scores, axis=1, keepdims=True)
            weights = jnp.exp(scores - top)
            e_hi, e_lo = split(weights)
            both = mm(e_hi, v_both[...], NN)
            close = both[:, :HD] + both[:, HD:] + mm(e_lo, v_both[:, :HD], NN)
            mass = jnp.broadcast_to(jnp.sum(weights, axis=1, keepdims=True), close.shape)
            place = pl.ds(pl.multiple_of(step * HEADS * BLOCK, HEADS * BLOCK), HEADS * BLOCK)
            near[n, place, :] = jnp.concatenate([close, mass], axis=1)

    def landing(n, step, j):
        s, g = n // KVL, n % KVL
        width = HEADS * HD
        return out.at[s, :, pl.ds(pl.multiple_of(j * QL + g * GROUP * HD + step * width, width), width)]

    def piece(n, step, j):
        width = HEADS * HD
        return mine.at[
            n, pl.ds(pl.multiple_of(j * ROWS, ROWS), ROWS), pl.ds(pl.multiple_of(step * width, width), width)
        ]

    def to_keeper(n, step, o):
        j, device = ring(o)
        return remote(
            piece(n, step, j), landing(n, step, kv), o_send.at[n, o, step], o_recv.at[n, kv, step], device
        )

    def to_self(n, step):
        return pltpu.make_async_copy(piece(n, step, kv), landing(n, step, kv), o_own.at[n, step])

    def from_ring(n, step, o):
        j = lax.rem(kv - o + 4, 4)
        landed = landing(n, step, j)
        return remote(landed, landed, o_send.at[n, o, step], o_recv.at[n, j, step], ring(o)[1])

    def finish(n):
        s, g = n // KVL, n % KVL
        for o in range(1, PLANE):
            from_plane(n, o, far, d_send, d_recv).wait_recv()
        total = jnp.concatenate([far[n, j] for j in range(PLANE)], axis=0)
        hi, lo = split(total)
        f_both[...] = jnp.concatenate([hi, lo], axis=0)
        norm = norms[n:n + 1, :]
        row = lax.broadcasted_iota(jnp.int32, (BLOCK, HD), 0)
        live = (row + anchor) >= starts_ref[s]

        @pl.loop(0, STEPS)
        def _(step):
            place = pl.ds(pl.multiple_of(step * HEADS * BLOCK, HEADS * BLOCK), HEADS * BLOCK)
            hi = p_hi[n, place, :]
            lo = p_lo[n, place, :]
            both = mm(hi, f_both[...], NT)
            distant = both[:, :HD] + both[:, HD:] + mm(lo, f_both[:HD, :], NT)
            seen = (hi.astype(F32) + lo.astype(F32)) * norm
            seen = jnp.sum(seen[:, :HALF] + seen[:, HALF:], axis=1, keepdims=True)
            seen = jnp.broadcast_to(seen, distant.shape)
            close = near[n, place, :]
            for k in range(HEADS):
                head = step * HEADS + k
                a = jax.nn.sigmoid(jnp.full((1, HD), mix_ref[g * GROUP + head], F32))
                part = slice(k * BLOCK, (k + 1) * BLOCK)
                top_part = a * close[part, :HD] + (1.0 - a) * distant[part, :HD]
                bottom = a * close[part, HD:] + (1.0 - a) * seen[part]
                result = jnp.where(live, top_part / jnp.where(live, bottom, 1.0), 0.0)
                mine[n, :, pl.ds(pl.multiple_of(head * HD, HD), HD)] = result
            for o in (2, 1, 3):
                to_keeper(n, step, o).start()
            to_self(n, step).start()

    for n in range(COMBOS):
        for t in range(2):
            loads_own[n, t].wait()
        shift(n).start()
    load_km.wait()
    n_tx[...] = jnp.zeros((8, FEAT), F32)
    window_own(0)
    query_features(0)
    state(0)
    window_prev(0)
    window_own(1)
    state(1)
    state(2)
    window_forward(0)
    state(3)
    norm_start()
    owner_total(0)
    window_prev(1)
    window_relay_same(0)
    window_relay_other(0)
    owner_total(1)
    window_own(2)
    owner_total(2)
    window_forward(1)
    owner_total(3)
    window_prev(2)
    norm_total()
    query_features(1)
    window_relay_same(1)
    window_relay_other(1)
    owner_prefix(0)
    window_forward(2)
    window_own(3)
    window_prev(3)
    owner_prefix(1)
    norm_finish()
    attend_near(0)
    owner_prefix(2)
    finish(0)
    window_relay_same(2)
    window_relay_other(2)
    window_forward(3)
    attend_near(1)
    owner_prefix(3)
    finish(1)
    window_relay_same(3)
    window_relay_other(3)
    attend_near(2)
    finish(2)
    attend_near(3)
    finish(3)

    for n in range(COMBOS):
        shift(n).wait_send()
        to_partner(n, own).wait_send()
        for o in (1, 3):
            to_line(n, o, own).wait_send()
            forward(n, o).wait_send()
        relay_same(n).wait_send()
        relay_other(n).wait_send()
        for o in range(1, PLANE):
            to_owner(n, o).wait_send()
            to_reader(n, o).wait_send()
        for o in range(1, PLANES - 1):
            @pl.when((z > 0) & (z + o < PLANES))
            def _():
                to_later(n, o).wait_send()
    for o in range(1, PLANE):
        norm_to_plane(o).wait_send()
    for o in range(1, PLANES - 1):
        @pl.when((z > 0) & (z + o < PLANES))
        def _():
            norm_to_later(o).wait_send()
    for n in range(COMBOS):
        @pl.loop(0, STEPS)
        def _(step):
            to_self(n, step).wait()
            for o in range(1, 4):
                to_keeper(n, step, o).wait_send()
                from_ring(n, step, o).wait_recv()


def on_device(queries, keys, values, query_maps, key_maps, mix, window_blocks, starts):
    smem = pl.BlockSpec(memory_space=pltpu.SMEM)
    hbm = pl.BlockSpec(memory_space=pltpu.HBM)
    dma = pltpu.SemaphoreType.DMA
    vmem = pltpu.VMEM
    pieces = (COMBOS, PLANE, PIECE, FEAT)
    return pl.pallas_call(
        kernel,
        out_shape=jax.ShapeDtypeStruct((SEQS, ROWS, 4 * QL), F32),
        in_specs=[smem, smem, smem] + [hbm] * 5,
        out_specs=pl.BlockSpec(memory_space=pl.ANY),
        scratch_shapes=[
            vmem((COMBOS, BLOCK, GROUP * HD), F32),
            vmem((KVL * GROUP, HD, HALF), F32),
            vmem((KVL, HD, HALF), F32),
            vmem((COMBOS, 2, BLOCK, HD), F32),
            vmem((COMBOS, 2, BLOCK, HD), F32),
            vmem((COMBOS, PLANE, 2, BLOCK, HD), F32),
            vmem(pieces, F32),
            vmem(pieces, F32),
            vmem((COMBOS, PIECE, FEAT), F32),
            vmem(pieces, F32),
            vmem(pieces, F32),
            vmem(pieces, F32),
            vmem((COMBOS, GROUP * BLOCK, FEAT), BF16),
            vmem((COMBOS, GROUP * BLOCK, FEAT), BF16),
            vmem((COMBOS, GROUP * BLOCK, 2 * HD), F32),
            vmem((COMBOS, BLOCK, GROUP * HD), F32),
            vmem((WIN, 2 * HD), BF16),
            vmem((WIN, 2 * HD), BF16),
            vmem((WIN, 2 * HD), BF16),
            vmem((2 * HD, FEAT), BF16),
            vmem((8, FEAT), F32),
            vmem((PLANE, 8, FEAT), F32),
            vmem((8, FEAT), F32),
            vmem((PLANES, 8, FEAT), F32),
            vmem((8, FEAT), F32),
            dma((COMBOS, 2)), dma((COMBOS,)), dma((KVL,)), dma((1,)), dma((COMBOS,)), dma((COMBOS,)),
            dma((COMBOS, 7)), dma((COMBOS, 8)),
            dma((COMBOS, 8)), dma((COMBOS, 8)), dma((COMBOS, 8)), dma((COMBOS, 8)), dma((COMBOS, 8)), dma((COMBOS, 8)),
            dma((COMBOS, 4, STEPS)), dma((COMBOS, 4, STEPS)), dma((COMBOS, STEPS)),
            dma((8,)), dma((8,)), dma((8,)), dma((8,)),
        ],
        name="hybrid",
        compiler_params=pltpu.CompilerParams(
            collective_id=0, has_side_effects=True, vmem_limit_bytes=61 << 20
        ),
    )(starts, window_blocks.T, mix, queries, keys, values, query_maps, key_maps)


def solution(mesh):
    torus = Mesh(mesh.devices.reshape(8, 2, 4, 2, 2), ("ctx_0", "ctx_1", "ctx_2", "kv_0", "kv_1"))
    in_specs = (
        P(None, CTX, KV),
        P(None, CTX, KV),
        P(None, CTX, KV),
        P(KV, None, None),
        P(KV, None, None),
        P(KV),
        P(None, CTX),
        P(),
    )
    out_specs = P(None, CTX_KV, None)
    return jax.shard_map(
        on_device, mesh=torus, in_specs=in_specs, out_specs=out_specs, check_vma=False
    )
```
